32 devices in a mesh: groups: 2 (over y), gx: 4 (over z), gy: 2 (over x), gz: 2 (over core).
Axes of the slice: x: 2, y: 2, z: 4, core: 2. Of those that a mesh axis runs over, the one named last changes fastest.
Arguments:
- polar_angle: float32 [16, 512, 256], P('gz', ('groups', 'gx'), 'gy'), parts along dimension 1, may hold values from -3.140625 to 3.140625
- azimuth: float32 [16, 512, 256], P('gz', ('groups', 'gx'), 'gy'), parts along dimension 1, may hold values from -3.140625 to 3.140625
- classes: int32 [6, 16, 512, 256], P(None, 'gz', ('groups', 'gx'), 'gy'), parts along dimension 2, may hold values from 0 to 7, as said below
- exchange_table: float32 [8], replicated, may hold values from 0.3 to 1.5
Outputs:
- spins_final: float32 [3, 16, 512, 256], P(None, 'gz', ('groups', 'gx'), 'gy'), parts along dimension 2
- modes_mid: float32 [32, 6144], P(('groups', 'gx')), parts along dimension 0
- modes_end: float32 [32, 6144], P(('groups', 'gx')), parts along dimension 0
The draws below stay inside these ranges and needn't reach their ends.
There are 2 independent parts, one for each index of `groups`. The reference program is written for one: setup_inputs(seed, part) draws one part's arguments, and reference() takes and returns one part's arrays. A program takes and returns all parts, laid end to end along the dimension named above; an argument that names none is the same for every part. Nothing has to cross between parts.
Inputs may be any that keep to these rules, and one draw needn't show every extreme that they name: `classes`: entry 3 + d of a site equals entry d of its lower neighbour along direction d (periodically), so every bond has one class seen from both ends.
All inputs are finite; a program needn't handle non-finite values.
Results may differ from the reference program's by a relative error of at most 0.0001.
Values sent between devices are 32-bit elements; how exact they have to be, the bound alone decides.
A program may use at most 128 MiB of HBM per device.

```python
import math
import jax
import jax.numpy as jnp
from jax import lax

KX = 32
KY = 32
NCLASS = 8
STEPS = 4
NX = 256
NY = 256
NZ = 16


def draw_classes(key, part):
    upper = jax.random.randint(key, (3, NZ, NX, NY), 0, NCLASS).astype(jnp.int32)
    lower = jnp.stack([jnp.roll(upper[0], 1, axis=1), jnp.roll(upper[1], 1, axis=2), jnp.roll(upper[2], 1, axis=0)])
    return jnp.concatenate([upper, lower], 0).astype(jnp.int32)


def setup_inputs(seed: int = 0, part: int = 0) -> dict:
    key_list = jax.random.split(jax.random.key(seed), 5)
    part_splits = jax.random.split(jax.random.fold_in(key_list[4], part), 5)
    return {
        "polar_angle": jnp.clip(jax.random.uniform(part_splits[0], (NZ, NX, NY), jnp.float32, -3.140625, 3.140625), -3.140625, 3.140625),
        "azimuth": jnp.clip(jax.random.uniform(part_splits[1], (NZ, NX, NY), jnp.float32, -3.140625, 3.140625), -3.140625, 3.140625),
        "classes": draw_classes(jax.random.fold_in(jax.random.fold_in(key_list[4], part), 71), part),
        "exchange_table": jnp.clip(jax.random.uniform(key_list[3], (NCLASS,), jnp.float32, 0.3, 1.5), 0.3, 1.5),
    }


time_step = 0.1
damping = 0.1


def cross_three(first, second):
    return jnp.stack([first[1] * second[2] - first[2] * second[1],
                      first[2] * second[0] - first[0] * second[2],
                      first[0] * second[1] - first[1] * second[0]])


def velocity(spin_field, coupling, neighbours):
    local_field = coupling[0][None] * neighbours[0]
    for direction in range(1, 6):
        local_field = local_field + coupling[direction][None] * neighbours[direction]
    torque = cross_three(spin_field, local_field)
    return -torque - damping * cross_three(spin_field, torque)


def rolled(spin_field):
    return [jnp.roll(spin_field, -1, 2), jnp.roll(spin_field, -1, 3), jnp.roll(spin_field, -1, 1),
            jnp.roll(spin_field, 1, 2), jnp.roll(spin_field, 1, 3), jnp.roll(spin_field, 1, 1)]


def heun_step(spin_field, coupling):
    slope_first = velocity(spin_field, coupling, rolled(spin_field))
    predicted = spin_field + time_step * slope_first
    slope_second = velocity(predicted, coupling, rolled(predicted))
    return spin_field + (0.5 * time_step) * (slope_first + slope_second)


def phase_table(wave_count, length, total_length):
    position = jnp.arange(length, dtype=jnp.int32)
    numbers = jnp.arange(wave_count, dtype=jnp.int32)
    index = (position[:, None] * numbers[None, :]) % total_length
    phase = index.astype(jnp.float32) * (2.0 * math.pi / total_length)
    return jnp.cos(phase), jnp.sin(phase)


def project(spin_field, x_table, y_table, z_cos, z_sin, scale):
    depth, wide_x, wide_y = spin_field.shape[1:]
    along_y = jnp.dot(spin_field.reshape(-1, wide_y), y_table, precision=lax.Precision.HIGHEST,
                      preferred_element_type=jnp.float32).reshape(3, depth, wide_x, 2 * KY)
    along_x = jnp.einsum('czxk,xm->czmk', along_y, x_table, precision=lax.Precision.HIGHEST)
    even_even = along_x[:, :, :KX, :KY]
    even_odd = along_x[:, :, :KX, KY:]
    odd_even = along_x[:, :, KX:, :KY]
    odd_odd = along_x[:, :, KX:, KY:]
    cosine_part = even_even - odd_odd
    sine_part = odd_even + even_odd
    hp = lax.Precision.HIGHEST
    real_part = jnp.einsum('czab,zk->kcab', cosine_part, z_cos, precision=hp) - jnp.einsum('czab,zk->kcab', sine_part, z_sin, precision=hp)
    imag_part = -(jnp.einsum('czab,zk->kcab', sine_part, z_cos, precision=hp) + jnp.einsum('czab,zk->kcab', cosine_part, z_sin, precision=hp))
    stacked = jnp.stack([real_part, imag_part], 1) * scale
    return stacked.reshape(z_cos.shape[1], -1)


def reference(polar_angle, azimuth, classes, exchange_table):
    spin_field = jnp.stack([jnp.sin(polar_angle) * jnp.cos(azimuth),
                            jnp.sin(polar_angle) * jnp.sin(azimuth),
                            jnp.cos(polar_angle)])
    coupling = jnp.take(exchange_table, classes)
    x_cos, x_sin = phase_table(KX, NX, NX)
    y_cos, y_sin = phase_table(KY, NY, NY)
    z_cos, z_sin = phase_table(NZ, NZ, NZ)
    x_table = jnp.concatenate([x_cos, x_sin], 1)
    y_table = jnp.concatenate([y_cos, y_sin], 1)
    scale = float(NX * NY * NZ) ** -0.5
    modes_mid = None
    for turn_index in range(STEPS):
        spin_field = heun_step(spin_field, coupling)
        if turn_index == 1:
            modes_mid = project(spin_field, x_table, y_table, z_cos, z_sin, scale)
    modes_end = project(spin_field, x_table, y_table, z_cos, z_sin, scale)
    return spin_field, modes_mid, modes_end
```

```python
import functools
import math

import jax
import jax.numpy as jnp
import numpy as np
from jax import lax
from jax.experimental import pallas as pl
from jax.experimental.pallas import tpu as pltpu
from jax.sharding import PartitionSpec as P

KX = 32
KY = 32
STEPS = 4
HALO = 8
MESH = pl.DeviceIdType.MESH

time_step = 0.1
damping = 0.1
HALF_SINE = (0.4999999978578703, -0.02083332246217966, 0.00026040783166918343, -1.5475817235376e-06,
             5.0882140435283864e-09)
HALF_COSINE = (0.9999999997798975, -0.12499999839235146, 0.0026041647630212603, -2.1700563804658615e-05,
               9.671927783275375e-08, -2.5440497387766775e-10)


def horner(coefficients, square):
    total = coefficients[-1]
    for value in coefficients[-2::-1]:
        total = total * square + value
    return total


def sin_cos(angle):
    square = angle * angle
    half_sine = angle * horner(HALF_SINE, square)
    half_cosine = horner(HALF_COSINE, square)
    twice = half_sine + half_sine
    return twice * half_cosine, 1.0 - twice * half_sine


def spins_of(polar, azimuth):
    sine_polar, cosine_polar = sin_cos(polar)
    sine_azimuth, cosine_azimuth = sin_cos(azimuth)
    scaled = sine_polar * damping
    return scaled * cosine_azimuth, scaled * sine_azimuth, cosine_polar * damping


def descent(spin, field):
    s0, s1, s2 = spin
    h0, h1, h2 = field
    w0 = h0 + (s1 * h2 - s2 * h1)
    w1 = h1 + (s2 * h0 - s0 * h2)
    w2 = h2 + (s0 * h1 - s1 * h0)
    return s1 * w2 - s2 * w1, s2 * w0 - s0 * w2, s0 * w1 - s1 * w0


def evolve_kernel(sizes, polar_in, azimuth_in, classes_in, table_ref, mid_ref, end_ref,
                  polar_ref, azimuth_ref, classes_ref, S, Q, J, GS, GQ, GJ, OS, OQ, OJ,
                  low, high, lowk, highk, pack, left_pack, right_pack, out,
                  xs, xr, ys, yr, zs, zr, gs, gr, osem, isem):
    nx, ny, nz = sizes
    depth, wide, lanes = polar_ref.shape
    ext = wide + 2 * HALO
    tiles = ext // 8
    inner = wide // 8
    group = 2 * HALO
    me_x, me_y, me_z = lax.axis_index("gx"), lax.axis_index("gy"), lax.axis_index("gz")

    def at(axis, me, n, step):
        return {axis: lax.rem(me + (step + n), n)}

    x_left, x_right = at("gx", me_x, nx, -1), at("gx", me_x, nx, 1)
    y_left, y_right = at("gy", me_y, ny, -1), at("gy", me_y, ny, 1)
    z_down, z_up = at("gz", me_z, nz, -1), at("gz", me_z, nz, 1)
    sides = [y_right] if ny == 2 else [y_right, y_left]

    fetches = [
        pltpu.make_async_copy(polar_in, polar_ref, isem.at[0]),
        pltpu.make_async_copy(azimuth_in, azimuth_ref, isem.at[1]),
        pltpu.make_async_copy(classes_in.at[pl.ds(0, 3)], classes_ref.at[pl.ds(0, 3)], isem.at[2]),
        pltpu.make_async_copy(classes_in.at[4], classes_ref.at[3], isem.at[3]),
        pltpu.make_async_copy(classes_in.at[5, 0], classes_ref.at[4, 0], isem.at[4]),
    ]
    for copy in fetches:
        copy.start()
    barrier = pltpu.get_barrier_semaphore()
    friends = [x_left, x_right, z_up] + sides + [{**x, **y} for x in (x_left, x_right) for y in sides]
    for who in friends:
        pl.semaphore_signal(barrier, inc=1, device_id=who, device_id_type=MESH)
    pl.semaphore_wait(barrier, len(friends))

    def remote(src, dst, send, recv, who):
        return pltpu.make_async_remote_copy(
            src_ref=src, dst_ref=dst, send_sem=send, recv_sem=recv, device_id=who, device_id_type=MESH
        )

    top = pl.ds(wide - HALO, HALO)
    bottom = pl.ds(0, HALO)
    x_copies = []
    for rows, halo, kinds, who in ((top, low, lowk, x_right), (bottom, high, highk, x_left)):
        for src, dst in (
            (polar_in.at[:, rows, :], halo.at[0]),
            (azimuth_in.at[:, rows, :], halo.at[1]),
            (classes_in.at[pl.ds(0, 3), :, rows, :], kinds.at[pl.ds(0, 3)]),
            (classes_in.at[5, 0, rows, :], kinds.at[3, 0]),
        ):
            i = len(x_copies)
            x_copies.append(remote(src, dst, xs.at[i], xr.at[i], who))
    for copy in x_copies:
        copy.start()

    lane = lax.broadcasted_iota(jnp.int32, (8, lanes), 1)
    group_of = lane // group
    place = lane % group
    ratio = time_step / damping
    table = jnp.zeros((8, lanes), jnp.float32)
    for i in range(table_ref.shape[0]):
        table = jnp.where(lane == i, table_ref[i] * ratio, table)

    def lookup(kinds):
        return jnp.take_along_axis(table, kinds, axis=1, mode="promise_in_bounds")

    for f in range(5):
        for r in range(inner):
            pack[f, pl.ds(8 * r, 8), :] = jnp.zeros((8, lanes), jnp.float32)
    for copy in fetches:
        copy.wait()

    def own_first(z, carry):
        mine = group_of == z
        mirror = (group * z + HALO - 1 + lanes - lane) % lanes
        for r in range(inner):
            rows = pl.ds(8 * r, 8)
            values = [polar_ref[z, rows, :], azimuth_ref[z, rows, :]]
            for d in range(3):
                value = lookup(classes_ref[d, z, rows, :])
                J[d, z + 1, pl.ds(HALO + 8 * r, 8), :] = value
                values.append(value)
            for f, value in enumerate(values):
                turned = jnp.take_along_axis(value, mirror, axis=1, mode="promise_in_bounds")
                pack[f, rows, :] = jnp.where(mine, turned, pack[f, rows, :])
        return carry

    lax.fori_loop(0, depth, own_first, 0)

    y_copies = []
    for side, (who, target) in enumerate(zip(sides, (left_pack, right_pack))):
        for part, (src, dst, to) in enumerate((
            (top, pl.ds(0, HALO), {**x_right, **who}),
            (bottom, pl.ds(HALO + wide, HALO), {**x_left, **who}),
            (pl.ds(0, wide), pl.ds(HALO, wide), who),
        )):
            i = 3 * side + part
            y_copies.append(remote(pack.at[:, src, :], target.at[:, dst, :], ys.at[i], yr.at[i], to))
    for copy in y_copies:
        copy.start()

    def own_second(z, carry):
        for r in range(inner):
            rows = pl.ds(8 * r, 8)
            spin = spins_of(polar_ref[z, rows, :], azimuth_ref[z, rows, :])
            for c in range(3):
                S[c, z + 1, pl.ds(HALO + 8 * r, 8), :] = spin[c]
            J[3, z + 1, pl.ds(HALO + 8 * r, 8), :] = lookup(classes_ref[3, z, rows, :])
        return carry

    lax.fori_loop(0, depth, own_second, 0)
    for r in range(inner):
        J[2, 0, pl.ds(HALO + 8 * r, 8), :] = lookup(classes_ref[4, 0, pl.ds(8 * r, 8), :])
    for copy in x_copies:
        copy.wait()

    def edges(z, carry):
        for halo, kinds, row in ((low, lowk, 0), (high, highk, HALO + wide)):
            spin = spins_of(halo[0, z], halo[1, z])
            for c in range(3):
                S[c, z + 1, pl.ds(row, 8), :] = spin[c]
            for d in range(3):
                J[d, z + 1, pl.ds(row, 8), :] = lookup(kinds[d, z])
        return carry

    lax.fori_loop(0, depth, edges, 0)
    J[2, 0, pl.ds(0, 8), :] = lookup(lowk[3, 0])
    J[2, 0, pl.ds(HALO + wide, 8), :] = lookup(highk[3, 0])

    def z_copies(field, base):
        return [
            remote(field.at[:, 1], field.at[:, depth + 1], zs.at[base], zr.at[base], z_down),
            remote(field.at[:, depth], field.at[:, 0], zs.at[base + 1], zr.at[base + 1], z_up),
        ]

    def g_copy(ghost, other, base):
        return remote(ghost, other, gs.at[base], gr.at[base], z_up)

    for copy in z_copies(S, 0):
        copy.start()
    for copy in y_copies:
        copy.wait()
    from_right = left_pack if ny == 2 else right_pack

    def ghosts(r, carry):
        rows = pl.ds(pl.multiple_of(8 * r, 8), 8)
        fields = [jnp.where(place >= HALO, left_pack[f, rows, :], from_right[f, rows, :]) for f in range(5)]
        spin = spins_of(fields[0], fields[1])
        for c in range(3):
            GS[c, rows, :] = spin[c]
        for d in range(3):
            GJ[d, rows, :] = fields[2 + d]
        edge = jnp.zeros((8, lanes), jnp.float32)
        for z in range(depth):
            edge = jnp.where(group_of == z, pltpu.roll(J[1, z + 1, rows, :], group * z + HALO, 1), edge)
        GJ[3, rows, :] = jnp.where(place == HALO - 1, edge, pltpu.roll(fields[3], lanes - 1, 1))
        return carry

    lax.fori_loop(0, tiles, ghosts, 0)
    g_copy(GS, OS, 0).start()
    g_copy(GJ.at[2], OJ, 2).start()

    def corners(z, carry):
        for row in (0, HALO + wide):
            rows = pl.ds(row, 8)
            outside = pltpu.roll(GJ[1, rows, :], lanes - (group * z + HALO), 1)
            J[3, z + 1, rows, :] = jnp.where(lane == 0, outside, pltpu.roll(J[1, z + 1, rows, :], 1, 1))
        return carry

    lax.fori_loop(0, depth, corners, 0)

    def x_pair(ref, r, value):
        ahead = ref[pl.ds(8 * r + 1, 8), :] if r < tiles - 1 else pltpu.roll(value, 7, 0)
        behind = ref[pl.ds(8 * r - 1, 8), :] if r > 0 else pltpu.roll(value, 1, 0)
        return ahead, behind

    def plane(F, G, z, finish, rows_of):
        up_shift = lanes - (group * z + HALO)
        for r in rows_of:
            rows = pl.ds(8 * r, 8)
            c0, c1, c2, c4 = (J[d, z + 1, rows, :] for d in range(4))
            c3 = J[0, z + 1, pl.ds(8 * r - 1, 8), :] if r > 0 else pltpu.roll(c0, 1, 0)
            c5 = J[2, z, rows, :]
            spin, field = [], []
            for c in range(3):
                M = F[c, z + 1, rows, :]
                ahead, behind = x_pair(F.at[c, z + 1], r, M)
                U = pltpu.roll(G[c, rows, :], up_shift, 1)
                right = jnp.where(lane == lanes - 1, U, pltpu.roll(M, lanes - 1, 1))
                left = jnp.where(lane == 0, U, pltpu.roll(M, 1, 1))
                total = (c0 * ahead + c3 * behind) + (c2 * F[c, z + 2, rows, :] + c5 * F[c, z, rows, :])
                total = total + (c1 * right + c4 * left)
                spin.append(M)
                field.append(total)
            finish(spin, descent(spin, field), z, rows)

    def ghost_pass(F, G, other, finish):
        for r in range(tiles):
            rows = pl.ds(8 * r, 8)
            c0, c1, c2, c4 = (GJ[d, rows, :] for d in range(4))
            c3 = GJ[0, pl.ds(8 * r - 1, 8), :] if r > 0 else pltpu.roll(c0, 1, 0)
            c5 = pltpu.roll(jnp.where(lane < lanes - group, c2, OJ[rows, :]), group, 1)
            spin, field = [], []
            for c in range(3):
                M = G[c, rows, :]
                O = other[c, rows, :]
                I = M
                for z in range(depth):
                    I = jnp.where(group_of == z, pltpu.roll(F[c, z + 1, rows, :], group * z + HALO, 1), I)
                ahead, behind = x_pair(G.at[c], r, M)
                right = jnp.where(place == HALO, I, pltpu.roll(M, 1, 1))
                left = jnp.where(place == HALO - 1, I, pltpu.roll(M, lanes - 1, 1))
                above = pltpu.roll(jnp.where(lane >= group, M, O), lanes - group, 1)
                below = pltpu.roll(jnp.where(lane < lanes - group, M, O), group, 1)
                total = (c0 * ahead + c3 * behind) + (c2 * above + c5 * below)
                total = total + (c1 * right + c4 * left)
                spin.append(M)
                field.append(total)
            finish(spin, descent(spin, field), rows)

    def predict(spin, change, z, rows):
        for c in range(3):
            Q[c, z + 1, rows, :] = spin[c] - change[c]

    def predict_ghost(spin, change, rows):
        for c in range(3):
            GQ[c, rows, :] = spin[c] - change[c]

    def correct(spin, change, z, rows):
        for c in range(3):
            S[c, z + 1, rows, :] = 0.5 * (S[c, z + 1, rows, :] + (spin[c] - change[c]))

    def correct_ghost(spin, change, rows):
        for c in range(3):
            GS[c, rows, :] = 0.5 * (GS[c, rows, :] + (spin[c] - change[c]))

    def stage(F, G, O, base, finish, finish_ghost, send_main, send_ghost, first=None):
        every = range(tiles)

        def inside(i, carry):
            plane(F, G, 2 * i + 1, finish, every)
            plane(F, G, 2 * i + 2, finish, every)
            return carry

        lax.fori_loop(0, (depth - 2) // 2, inside, 0)
        for copy in z_copies(F, 2 * base):
            copy.wait()
        plane(F, G, 0, finish, every)
        plane(F, G, depth - 1, finish, every)
        send_main()
        g_copy(G, O, base).wait()
        if first is not None:
            first()
        ghost_pass(F, G, O, finish_ghost)
        send_ghost()

    def publish(target, sem):
        copy = pltpu.make_async_copy(out, target, sem)

        def scaled(z, carry):
            for c in range(3):
                for r in range(inner):
                    out[c, z, pl.ds(8 * r, 8), :] = S[c, z + 1, pl.ds(HALO + 8 * r, 8), :] * (1.0 / damping)
            return carry

        lax.fori_loop(0, depth, scaled, 0)
        return copy

    def step(turn, carry):
        def send_q():
            for copy in z_copies(Q, 2):
                copy.start()

        def send_s():
            @pl.when(turn < STEPS - 1)
            def _():
                for copy in z_copies(S, 0):
                    copy.start()

        def send_gs():
            @pl.when(turn < STEPS - 1)
            def _():
                g_copy(GS, OS, 0).start()

        def couplings():
            @pl.when(turn == 0)
            def _():
                g_copy(GJ.at[2], OJ, 2).wait()

        stage(S, GS, OS, 0, predict, predict_ghost, send_q, lambda: g_copy(GQ, OQ, 1).start(), couplings)

        @pl.when(turn == 2)
        def _():
            pltpu.make_async_copy(out, mid_ref, osem.at[0]).wait()

        stage(Q, GQ, OQ, 1, correct, correct_ghost, send_s, send_gs)

        @pl.when(turn == 1)
        def _():
            publish(mid_ref, osem.at[0]).start()

        return carry

    lax.fori_loop(0, STEPS, step, 0)
    final = publish(end_ref, osem.at[0])
    final.start()
    final.wait()


def evolve(polar_angle, azimuth, classes, exchange_table):
    depth, wide, lanes = polar_angle.shape
    sizes = (lax.axis_size("gx"), lax.axis_size("gy"), lax.axis_size("gz"))
    assert sizes[2] == 2 and depth * 2 * HALO == lanes
    ext = wide + 2 * HALO
    f32, i32 = jnp.float32, jnp.int32
    out = jax.ShapeDtypeStruct((3, depth, wide, lanes), f32)
    hbm = pl.BlockSpec(memory_space=pltpu.HBM)
    anywhere = pl.BlockSpec(memory_space=pl.ANY)
    V = pltpu.VMEM
    D = pltpu.SemaphoreType.DMA
    return pl.pallas_call(
        functools.partial(evolve_kernel, sizes),
        out_shape=(out, out),
        in_specs=[hbm, hbm, hbm, pl.BlockSpec(memory_space=pltpu.SMEM)],
        out_specs=(anywhere, anywhere),
        scratch_shapes=[
            V((depth, wide, lanes), f32), V((depth, wide, lanes), f32), V((5, depth, wide, lanes), i32),
            V((3, depth + 2, ext, lanes), f32), V((3, depth + 2, ext, lanes), f32),
            V((4, depth + 1, ext, lanes), f32),
            V((3, ext, lanes), f32), V((3, ext, lanes), f32), V((4, ext, lanes), f32),
            V((3, ext, lanes), f32), V((3, ext, lanes), f32), V((ext, lanes), f32),
            V((2, depth, HALO, lanes), f32), V((2, depth, HALO, lanes), f32),
            V((4, depth, HALO, lanes), i32), V((4, depth, HALO, lanes), i32),
            V((5, wide, lanes), f32), V((5, ext, lanes), f32), V((5, ext, lanes), f32),
            V((3, depth, wide, lanes), f32),
            D((8,)), D((8,)), D((6,)), D((6,)), D((4,)), D((4,)), D((3,)), D((3,)), D((1,)), D((5,)),
        ],
        compiler_params=pltpu.CompilerParams(collective_id=0, has_side_effects=True, vmem_limit_bytes=65200000),
        name="evolve",
    )(polar_angle, azimuth, classes, exchange_table)


def phase_table(wave_count, total_length):
    index = np.arange(total_length)[:, None] * np.arange(wave_count)[None, :] % total_length
    phase = index * (2.0 * math.pi / total_length)
    return np.cos(phase).astype(np.float32), np.sin(phase).astype(np.float32)


def exact_dot(a, b):
    return jnp.dot(a, b, precision=lax.Precision.HIGHEST, preferred_element_type=jnp.float32)


def modes_kernel(sizes, scale, mid_ref, end_ref, x_in, y_in, cos_ref, sin_ref, out_ref,
                 x_ref, y_ref, T, R, Z, D, DR, E, F, zs, zr, xs, xr, ys, yr, fs, fr, isem):
    nx, ny, nz = sizes
    depth, wide, lanes = mid_ref.shape[1:]
    owned = D.shape[2]
    half = KX // nz
    me_x, me_y, me_z = lax.axis_index("gx"), lax.axis_index("gy"), lax.axis_index("gz")
    peers_x = [{"gx": lax.rem(me_x + o, nx)} for o in range(1, nx)]
    peers_y = [{"gy": lax.rem(me_y + o, ny)} for o in range(1, ny)]
    twin = {"gz": 1 - me_z}
    fetches = [
        pltpu.make_async_copy(x_in.at[me_x], x_ref, isem.at[0]),
        pltpu.make_async_copy(y_in.at[me_y], y_ref, isem.at[1]),
    ]
    for copy in fetches:
        copy.start()

    barrier = pltpu.get_barrier_semaphore()
    for who in peers_x + peers_y + [twin]:
        pl.semaphore_signal(barrier, inc=1, device_id=who, device_id_type=MESH)
    pl.semaphore_wait(barrier, nx + ny - 1)

    def remote(src, dst, send, recv, who):
        return pltpu.make_async_remote_copy(
            src_ref=src, dst_ref=dst, send_sem=send, recv_sem=recv, device_id=who, device_id_type=MESH
        )

    lane = lax.broadcasted_iota(jnp.int32, (half, 4 * KY), 1)
    cosine_lane = (lane // KY) % 2 == 0
    for copy in fetches:
        copy.wait()
    table = x_ref[...]
    swaps, x_copies, y_copies, shares = [], [], [], []

    def transform(c):
        for z in range(depth):
            for turn, ref in enumerate((mid_ref, end_ref)):
                along_x = exact_dot(table, ref[c, z])
                T[pl.ds(z * KX, KX), pl.ds(2 * lanes * turn, lanes)] = along_x[:KX]
                T[pl.ds(z * KX, KX), pl.ds(2 * lanes * turn + lanes, lanes)] = along_x[KX:]
        parts = exact_dot(T[...], y_ref[...]).reshape(depth, nz, half, 4 * KY)
        for h in range(nz):
            R[h, c] = parts[:, h]
        swaps.append(remote(R.at[1 - me_z, c], Z.at[c], zs.at[c], zr.at[c], twin))
        swaps[c].start()

    def waves(c):
        swaps[c].wait()
        ones, twos = [], []
        for z in range(nz * depth):
            own = R[me_z, c, z] if z < depth else Z[c, z - depth]
            ones.append(own)
            twos.append(jnp.where(cosine_lane, -pltpu.roll(own, 3 * KY, 1), pltpu.roll(own, KY, 1)))

        def block_of(block, carry):
            for k in range(owned):
                total = None
                for z in range(nz * depth):
                    where_z = me_z * depth + z if z < depth else (1 - me_z) * depth + z - depth
                    wave = block * owned + k
                    term = cos_ref[wave, where_z] * ones[z] + sin_ref[wave, where_z] * twos[z]
                    total = term if total is None else total + term
                D[c, block, k] = total
            return carry

        lax.fori_loop(0, nx, block_of, 0)
        x_copies.append([
            remote(D.at[c, lax.rem(me_x + o, nx)], DR.at[c, o - 1], xs.at[c, o - 1], xr.at[c, o - 1], peers_x[o - 1])
            for o in range(1, nx)
        ])
        for copy in reversed(x_copies[c]):
            copy.start()

    def sum_x(c):
        for copy in x_copies[c]:
            copy.wait()
        total = D[c, me_x]
        for o in range(1, nx):
            total = total + DR[c, o - 1]
        E[c, me_y] = total
        y_copies.append([
            remote(E.at[c, me_y], E.at[c, me_y], ys.at[c, o - 1], yr.at[c, o - 1], peers_y[o - 1])
            for o in range(1, ny)
        ])
        for copy in y_copies[c]:
            copy.start()

    def sum_y(c):
        for copy in y_copies[c]:
            copy.wait()
        total = E[c, 0]
        for o in range(1, ny):
            total = total + E[c, o]
        F[c, me_z] = total * jnp.where(cosine_lane, scale, -scale)
        shares.append(remote(F.at[c, me_z], F.at[c, me_z], fs.at[c], fr.at[c], twin))
        shares[c].start()

    transform(0)
    transform(1)
    waves(0)
    transform(2)
    waves(1)
    waves(2)
    sum_x(0)
    sum_x(1)
    sum_y(0)
    sum_x(2)
    sum_y(1)
    sum_y(2)
    for c in range(3):
        shares[c].wait()
        out_ref[:, :, c] = F[c]


def modes(spin_mid, spin_end):
    depth, wide, lanes = spin_mid.shape[1:]
    sizes = nx, ny, nz = (lax.axis_size("gx"), lax.axis_size("gy"), lax.axis_size("gz"))
    total_z = depth * nz
    owned = total_z // nx
    half = KX // nz
    f32 = jnp.float32
    x_cos, x_sin = phase_table(KX, wide * nx)
    y_cos, y_sin = phase_table(KY, lanes * ny)
    z_cos, z_sin = phase_table(total_z, total_z)
    x_full = np.concatenate([x_cos, x_sin], 1).reshape(nx, wide, 2 * KX).transpose(0, 2, 1)
    y_pair = np.stack([
        np.concatenate([y_cos, y_sin], 1).reshape(ny, lanes, 2 * KY),
        np.concatenate([-y_sin, y_cos], 1).reshape(ny, lanes, 2 * KY),
    ], 1).reshape(ny, 2 * lanes, 2 * KY)
    y_full = np.zeros((ny, 4 * lanes, 4 * KY), np.float32)
    y_full[:, : 2 * lanes, : 2 * KY] = y_pair
    y_full[:, 2 * lanes :, 2 * KY :] = y_pair
    scale = float(wide * nx * lanes * ny * total_z) ** -0.5
    vmem = pl.BlockSpec(memory_space=pltpu.VMEM)
    smem = pl.BlockSpec(memory_space=pltpu.SMEM)
    hbm = pl.BlockSpec(memory_space=pltpu.HBM)
    V, DMA = pltpu.VMEM, pltpu.SemaphoreType.DMA
    width = 4 * KY
    out = pl.pallas_call(
        functools.partial(modes_kernel, sizes, scale),
        out_shape=jax.ShapeDtypeStruct((nz, owned, 3, half, width), f32),
        in_specs=[vmem, vmem, hbm, hbm, smem, smem],
        out_specs=vmem,
        scratch_shapes=[
            V((2 * KX, wide), f32), V((4 * lanes, width), f32),
            V((depth * KX, 4 * lanes), f32), V((nz, 3, depth, half, width), f32),
            V((3, depth, half, width), f32), V((3, nx, owned, half, width), f32),
            V((3, nx - 1, owned, half, width), f32), V((3, ny, owned, half, width), f32),
            V((3, nz, owned, half, width), f32),
            DMA((3,)), DMA((3,)), DMA((3, nx - 1)), DMA((3, nx - 1)), DMA((3, ny - 1)), DMA((3, ny - 1)),
            DMA((3,)), DMA((3,)), DMA((2,)),
        ],
        compiler_params=pltpu.CompilerParams(collective_id=1, has_side_effects=True, vmem_limit_bytes=32 * 1024 * 1024),
        name="modes",
    )(spin_mid, spin_end, jnp.asarray(x_full), jnp.asarray(y_full), jnp.asarray(z_cos.T), jnp.asarray(z_sin.T))
    out = out.reshape(nz, owned, 3, half, 2, 2, KY).transpose(4, 1, 5, 2, 0, 3, 6)
    return out.reshape(2, owned, -1)


def body(polar_angle, azimuth, classes, exchange_table):
    spin_mid, spin_end = evolve(polar_angle, azimuth, classes, exchange_table)
    both = modes(spin_mid, spin_end)
    return (spin_end, both[0], both[1])


def solution(mesh):
    return jax.shard_map(
        body,
        mesh=mesh,
        in_specs=(
            P("gz", ("groups", "gx"), "gy"),
            P("gz", ("groups", "gx"), "gy"),
            P(None, "gz", ("groups", "gx"), "gy"),
            P(),
        ),
        out_specs=(
            P(None, "gz", ("groups", "gx"), "gy"),
            P(("groups", "gx"), None),
            P(("groups", "gx"), None),
        ),
        check_vma=False,
    )
```

```python
import functools
import math

import jax
import jax.numpy as jnp
import numpy as np
from jax import lax
from jax.experimental import pallas as pl
from jax.experimental.pallas import tpu as pltpu
from jax.sharding import PartitionSpec as P

KX = 32
KY = 32
STEPS = 4
HALO = 8
MESH = pl.DeviceIdType.MESH

time_step = 0.1
damping = 0.1
HALF_SINE = (0.4999999978578703, -0.02083332246217966, 0.00026040783166918343, -1.5475817235376e-06,
             5.0882140435283864e-09)
HALF_COSINE = (0.9999999997798975, -0.12499999839235146, 0.0026041647630212603, -2.1700563804658615e-05,
               9.671927783275375e-08, -2.5440497387766775e-10)


def horner(coefficients, square):
    total = coefficients[-1]
    for value in coefficients[-2::-1]:
        total = total * square + value
    return total


def sin_cos(angle):
    square = angle * angle
    half_sine = angle * horner(HALF_SINE, square)
    half_cosine = horner(HALF_COSINE, square)
    twice = half_sine + half_sine
    return twice * half_cosine, 1.0 - twice * half_sine


def spins_of(polar, azimuth):
    sine_polar, cosine_polar = sin_cos(polar)
    sine_azimuth, cosine_azimuth = sin_cos(azimuth)
    scaled = sine_polar * damping
    return scaled * cosine_azimuth, scaled * sine_azimuth, cosine_polar * damping


def descent(spin, field):
    s0, s1, s2 = spin
    h0, h1, h2 = field
    w0 = h0 + (s1 * h2 - s2 * h1)
    w1 = h1 + (s2 * h0 - s0 * h2)
    w2 = h2 + (s0 * h1 - s1 * h0)
    return s1 * w2 - s2 * w1, s2 * w0 - s0 * w2, s0 * w1 - s1 * w0


def evolve_kernel(sizes, polar_in, azimuth_in, classes_in, y_in, x_in, z_in, table_ref, end_ref, mid_out, end_out,
                  polar_ref, azimuth_ref, classes_ref, S, Q, J, GS, GQ, GJ, OS, OQ, OJ,
                  low, high, lowk, highk, pack, left_pack, right_pack, out,
                  y_table, x_table, z_table, along_y, waves_xy, planes, twin_planes, sums, peer_sums, rows_sum, whole,
                  xs, xr, ys, yr, zs, zr, gs, gr, osem, isem, ts, tr, ps, pr, qs, qr, fs, fr):
    nx, ny, nz = sizes
    depth, wide, lanes = polar_ref.shape
    ext = wide + 2 * HALO
    tiles = ext // 8
    inner = wide // 8
    group = 2 * HALO
    me_x, me_y, me_z = lax.axis_index("gx"), lax.axis_index("gy"), lax.axis_index("gz")

    def at(axis, me, n, step):
        return {axis: lax.rem(me + (step + n), n)}

    x_left, x_right = at("gx", me_x, nx, -1), at("gx", me_x, nx, 1)
    y_left, y_right = at("gy", me_y, ny, -1), at("gy", me_y, ny, 1)
    z_down, z_up = at("gz", me_z, nz, -1), at("gz", me_z, nz, 1)
    sides = [y_right] if ny == 2 else [y_right, y_left]

    fetches = [
        pltpu.make_async_copy(polar_in, polar_ref, isem.at[0]),
        pltpu.make_async_copy(azimuth_in, azimuth_ref, isem.at[1]),
        pltpu.make_async_copy(classes_in.at[pl.ds(0, 3)], classes_ref.at[pl.ds(0, 3)], isem.at[2]),
        pltpu.make_async_copy(classes_in.at[4], classes_ref.at[3], isem.at[3]),
        pltpu.make_async_copy(classes_in.at[5, 0], classes_ref.at[4, 0], isem.at[4]),
    ]
    tables = [
        pltpu.make_async_copy(y_in.at[me_y], y_table, isem.at[5]),
        pltpu.make_async_copy(x_in.at[me_x], x_table, isem.at[6]),
        pltpu.make_async_copy(z_in.at[me_z], z_table, isem.at[7]),
    ]
    for copy in fetches + tables:
        copy.start()
    peers_x = [at("gx", me_x, nx, o) for o in range(1, nx)]
    peers_y = [at("gy", me_y, ny, o) for o in range(1, ny)]
    barrier = pltpu.get_barrier_semaphore()
    friends = peers_x + peers_y + [z_up] + [{**x, **y} for x in (x_left, x_right) for y in sides]
    for who in friends:
        pl.semaphore_signal(barrier, inc=1, device_id=who, device_id_type=MESH)
    pl.semaphore_wait(barrier, len(friends))

    def remote(src, dst, send, recv, who):
        return pltpu.make_async_remote_copy(
            src_ref=src, dst_ref=dst, send_sem=send, recv_sem=recv, device_id=who, device_id_type=MESH
        )

    top = pl.ds(wide - HALO, HALO)
    bottom = pl.ds(0, HALO)
    x_copies = []
    for rows, halo, kinds, who in ((top, low, lowk, x_right), (bottom, high, highk, x_left)):
        for src, dst in (
            (polar_in.at[:, rows, :], halo.at[0]),
            (azimuth_in.at[:, rows, :], halo.at[1]),
            (classes_in.at[pl.ds(0, 3), :, rows, :], kinds.at[pl.ds(0, 3)]),
            (classes_in.at[5, 0, rows, :], kinds.at[3, 0]),
        ):
            i = len(x_copies)
            x_copies.append(remote(src, dst, xs.at[i], xr.at[i], who))
    for copy in x_copies:
        copy.start()

    lane = lax.broadcasted_iota(jnp.int32, (8, lanes), 1)
    group_of = lane // group
    place = lane % group
    ratio = time_step / damping
    table = jnp.zeros((8, lanes), jnp.float32)
    for i in range(table_ref.shape[0]):
        table = jnp.where(lane == i, table_ref[i] * ratio, table)

    def lookup(kinds):
        return jnp.take_along_axis(table, kinds, axis=1, mode="promise_in_bounds")

    for f in range(5):
        for r in range(inner):
            pack[f, pl.ds(8 * r, 8), :] = jnp.zeros((8, lanes), jnp.float32)
    for copy in fetches:
        copy.wait()

    def own_first(z, carry):
        mine = group_of == z
        mirror = (group * z + HALO - 1 + lanes - lane) % lanes
        for r in range(inner):
            rows = pl.ds(8 * r, 8)
            values = [polar_ref[z, rows, :], azimuth_ref[z, rows, :]]
            for d in range(3):
                value = lookup(classes_ref[d, z, rows, :])
                J[d, z + 1, pl.ds(HALO + 8 * r, 8), :] = value
                values.append(value)
            for f, value in enumerate(values):
                turned = jnp.take_along_axis(value, mirror, axis=1, mode="promise_in_bounds")
                pack[f, rows, :] = jnp.where(mine, turned, pack[f, rows, :])
        return carry

    lax.fori_loop(0, depth, own_first, 0)

    y_copies = []
    for side, (who, target) in enumerate(zip(sides, (left_pack, right_pack))):
        for part, (src, dst, to) in enumerate((
            (top, pl.ds(0, HALO), {**x_right, **who}),
            (bottom, pl.ds(HALO + wide, HALO), {**x_left, **who}),
            (pl.ds(0, wide), pl.ds(HALO, wide), who),
        )):
            i = 3 * side + part
            y_copies.append(remote(pack.at[:, src, :], target.at[:, dst, :], ys.at[i], yr.at[i], to))
    for copy in y_copies:
        copy.start()

    def own_second(z, carry):
        for r in range(inner):
            rows = pl.ds(8 * r, 8)
            spin = spins_of(polar_ref[z, rows, :], azimuth_ref[z, rows, :])
            for c in range(3):
                S[c, z + 1, pl.ds(HALO + 8 * r, 8), :] = spin[c]
            J[3, z + 1, pl.ds(HALO + 8 * r, 8), :] = lookup(classes_ref[3, z, rows, :])
        return carry

    lax.fori_loop(0, depth, own_second, 0)
    for r in range(inner):
        J[2, 0, pl.ds(HALO + 8 * r, 8), :] = lookup(classes_ref[4, 0, pl.ds(8 * r, 8), :])
    for copy in x_copies:
        copy.wait()

    def edges(z, carry):
        for halo, kinds, row in ((low, lowk, 0), (high, highk, HALO + wide)):
            spin = spins_of(halo[0, z], halo[1, z])
            for c in range(3):
                S[c, z + 1, pl.ds(row, 8), :] = spin[c]
            for d in range(3):
                J[d, z + 1, pl.ds(row, 8), :] = lookup(kinds[d, z])
        return carry

    lax.fori_loop(0, depth, edges, 0)
    J[2, 0, pl.ds(0, 8), :] = lookup(lowk[3, 0])
    J[2, 0, pl.ds(HALO + wide, 8), :] = lookup(highk[3, 0])

    def z_copies(field, base):
        return [
            remote(field.at[:, 1], field.at[:, depth + 1], zs.at[base], zr.at[base], z_down),
            remote(field.at[:, depth], field.at[:, 0], zs.at[base + 1], zr.at[base + 1], z_up),
        ]

    def g_copy(ghost, other, base):
        return remote(ghost, other, gs.at[base], gr.at[base], z_up)

    for copy in z_copies(S, 0):
        copy.start()
    for copy in y_copies:
        copy.wait()
    from_right = left_pack if ny == 2 else right_pack

    def ghosts(r, carry):
        rows = pl.ds(pl.multiple_of(8 * r, 8), 8)
        fields = [jnp.where(place >= HALO, left_pack[f, rows, :], from_right[f, rows, :]) for f in range(5)]
        spin = spins_of(fields[0], fields[1])
        for c in range(3):
            GS[c, rows, :] = spin[c]
        for d in range(3):
            GJ[d, rows, :] = fields[2 + d]
        edge = jnp.zeros((8, lanes), jnp.float32)
        for z in range(depth):
            edge = jnp.where(group_of == z, pltpu.roll(J[1, z + 1, rows, :], group * z + HALO, 1), edge)
        GJ[3, rows, :] = jnp.where(place == HALO - 1, edge, pltpu.roll(fields[3], lanes - 1, 1))
        return carry

    lax.fori_loop(0, tiles, ghosts, 0)
    g_copy(GS, OS, 0).start()
    g_copy(GJ.at[2], OJ, 2).start()

    def corners(z, carry):
        for row in (0, HALO + wide):
            rows = pl.ds(row, 8)
            outside = pltpu.roll(GJ[1, rows, :], lanes - (group * z + HALO), 1)
            J[3, z + 1, rows, :] = jnp.where(lane == 0, outside, pltpu.roll(J[1, z + 1, rows, :], 1, 1))
        return carry

    lax.fori_loop(0, depth, corners, 0)

    def x_pair(ref, r, value):
        ahead = ref[pl.ds(8 * r + 1, 8), :] if r < tiles - 1 else pltpu.roll(value, 7, 0)
        behind = ref[pl.ds(8 * r - 1, 8), :] if r > 0 else pltpu.roll(value, 1, 0)
        return ahead, behind

    def plane(F, G, z, finish, rows_of):
        up_shift = lanes - (group * z + HALO)
        for r in rows_of:
            rows = pl.ds(8 * r, 8)
            c0, c1, c2, c4 = (J[d, z + 1, rows, :] for d in range(4))
            c3 = J[0, z + 1, pl.ds(8 * r - 1, 8), :] if r > 0 else pltpu.roll(c0, 1, 0)
            c5 = J[2, z, rows, :]
            spin, field = [], []
            for c in range(3):
                M = F[c, z + 1, rows, :]
                ahead, behind = x_pair(F.at[c, z + 1], r, M)
                U = pltpu.roll(G[c, rows, :], up_shift, 1)
                right = jnp.where(lane == lanes - 1, U, pltpu.roll(M, lanes - 1, 1))
                left = jnp.where(lane == 0, U, pltpu.roll(M, 1, 1))
                total = (c0 * ahead + c3 * behind) + (c2 * F[c, z + 2, rows, :] + c5 * F[c, z, rows, :])
                total = total + (c1 * right + c4 * left)
                spin.append(M)
                field.append(total)
            finish(spin, descent(spin, field), z, rows)

    def ghost_pass(F, G, other, finish):
        for r in range(tiles):
            rows = pl.ds(8 * r, 8)
            c0, c1, c2, c4 = (GJ[d, rows, :] for d in range(4))
            c3 = GJ[0, pl.ds(8 * r - 1, 8), :] if r > 0 else pltpu.roll(c0, 1, 0)
            c5 = pltpu.roll(jnp.where(lane < lanes - group, c2, OJ[rows, :]), group, 1)
            spin, field = [], []
            for c in range(3):
                M = G[c, rows, :]
                O = other[c, rows, :]
                I = M
                for z in range(depth):
                    I = jnp.where(group_of == z, pltpu.roll(F[c, z + 1, rows, :], group * z + HALO, 1), I)
                ahead, behind = x_pair(G.at[c], r, M)
                right = jnp.where(place == HALO, I, pltpu.roll(M, 1, 1))
                left = jnp.where(place == HALO - 1, I, pltpu.roll(M, lanes - 1, 1))
                above = pltpu.roll(jnp.where(lane >= group, M, O), lanes - group, 1)
                below = pltpu.roll(jnp.where(lane < lanes - group, M, O), group, 1)
                total = (c0 * ahead + c3 * behind) + (c2 * above + c5 * below)
                total = total + (c1 * right + c4 * left)
                spin.append(M)
                field.append(total)
            finish(spin, descent(spin, field), rows)

    def predict(spin, change, z, rows):
        for c in range(3):
            Q[c, z + 1, rows, :] = spin[c] - change[c]

    def predict_ghost(spin, change, rows):
        for c in range(3):
            GQ[c, rows, :] = spin[c] - change[c]

    def correct(spin, change, z, rows):
        for c in range(3):
            S[c, z + 1, rows, :] = 0.5 * (S[c, z + 1, rows, :] + (spin[c] - change[c]))

    def correct_ghost(spin, change, rows):
        for c in range(3):
            GS[c, rows, :] = 0.5 * (GS[c, rows, :] + (spin[c] - change[c]))

    def stage(F, G, O, base, finish, finish_ghost, send_main, send_ghost, first=None, every=range(tiles)):
        def inside(i, carry):
            plane(F, G, 2 * i + 1, finish, every)
            plane(F, G, 2 * i + 2, finish, every)
            return carry

        lax.fori_loop(0, (depth - 2) // 2, inside, 0)
        for copy in z_copies(F, 2 * base):
            copy.wait()
        plane(F, G, 0, finish, every)
        plane(F, G, depth - 1, finish, every)
        send_main()
        g_copy(G, O, base).wait()
        if finish_ghost is None:
            return
        if first is not None:
            first()
        ghost_pass(F, G, O, finish_ghost)
        send_ghost()

    def split(value):
        big = value.astype(jnp.bfloat16)
        return big, (value - big.astype(jnp.float32)).astype(jnp.bfloat16)

    def dot(a, b):
        return jnp.dot(a, b, preferred_element_type=jnp.float32)

    half = KX // nz
    quad = lanes // KY

    def transform(f, c):
        for z in range(depth):
            big, small = split(S[c, z + 1, pl.ds(HALO, wide), :])
            along_y[pl.ds(z * wide, wide), pl.ds(0, lanes)] = big
            along_y[pl.ds(z * wide, wide), pl.ds(lanes, lanes)] = small
        both = dot(along_y[...], y_table[...])
        both = both[:, :lanes] + both[:, lanes:]
        for z in range(0, depth, 2):
            parts = []
            for i in (z, z + 1):
                big, small = split(both[i * wide : (i + 1) * wide])
                parts.append(jnp.concatenate([big, small, big, small], 0))
            along_x = dot(x_table[...], jnp.concatenate(parts, 1))
            for i in range(2):
                mine = along_x[:, i * lanes : (i + 1) * lanes]
                waves_xy[pl.ds((z + i) * KX, KX), :] = mine[:KX] + pltpu.roll(mine[KX:], lanes // 2, 1)
        slot = lane // KY
        for h in range(nz):
            for j in range(half // quad):
                loads = [waves_xy[pl.ds(h * half + j * quad + k, depth, stride=KX), :] for k in range(quad)]
                for p in range(2):
                    total = None
                    for k, value in enumerate(loads):
                        turn = (k - p) % quad * KY
                        value = pltpu.roll(value, turn, 1) if turn else value
                        total = value if total is None else jnp.where(slot == k, value, total)
                    planes[f, h, c, pl.ds(p * depth, depth), pl.ds(j * lanes, lanes)] = total

    def swap(f, c):
        return remote(planes.at[f, 1 - me_z, c], twin_planes.at[f, c], ts.at[f, c], tr.at[f, c], z_up)

    def waves(f, c):
        stacked = jnp.concatenate([planes[f, me_z, c], twin_planes[f, c]], 0)
        big, small = split(stacked)
        result = dot(z_table[...], jnp.concatenate([big, small, big, small], 0))
        for b in range(nx):
            sums[f, c, b] = result[8 * b : 8 * b + 8]

    def x_sends(f, c):
        return [
            remote(sums.at[f, c, lax.rem(me_x + o, nx)], peer_sums.at[f, c, o - 1], ps.at[f, c, o - 1],
                   pr.at[f, c, o - 1], peers_x[o - 1])
            for o in range(1, nx)
        ]

    def y_sends(f, c):
        return [
            remote(rows_sum.at[f, c, me_y], rows_sum.at[f, c, me_y], qs.at[f, c, o - 1], qr.at[f, c, o - 1],
                   peers_y[o - 1])
            for o in range(1, ny)
        ]

    def share(f, c):
        return remote(whole.at[f, c, me_z], whole.at[f, c, me_z], fs.at[f, c], fr.at[f, c], z_up)

    def local_part(f):
        for c in range(3):
            transform(f, c)
            swap(f, c).start()

    def wave_part(f):
        for c in range(3):
            swap(f, c).wait()
            waves(f, c)
            for copy in reversed(x_sends(f, c)):
                copy.start()

    def x_part(f):
        for c in range(3):
            for copy in x_sends(f, c):
                copy.wait()
            total = sums[f, c, me_x]
            for o in range(1, nx):
                total = total + peer_sums[f, c, o - 1]
            rows_sum[f, c, me_y] = total
            for copy in y_sends(f, c):
                copy.start()

    def y_part(f):
        for c in range(3):
            for copy in y_sends(f, c):
                copy.wait()
            total = rows_sum[f, c, 0]
            for o in range(1, ny):
                total = total + rows_sum[f, c, o]
            whole[f, c, me_z] = total
            share(f, c).start()

    def last_part(f, target):
        owned = target.shape[0]
        for c in range(3):
            share(f, c).wait()
            for h in range(nz):
                for p in range(2):
                    start = (p * 3 + c) * KX * KY + h * half * KY
                    target[:, pl.ds(start, half * KY)] = whole[f, c, h, pl.ds(p * owned, owned), :]

    def send_q():
        for copy in z_copies(Q, 2):
            copy.start()

    def send_s():
        for copy in z_copies(S, 0):
            copy.start()

    def predict_stage(first=None):
        stage(S, GS, OS, 0, predict, predict_ghost, send_q, lambda: g_copy(GQ, OQ, 1).start(), first)

    def step(turn, carry):
        def couplings():
            @pl.when(turn == 0)
            def _():
                g_copy(GJ.at[2], OJ, 2).wait()

        predict_stage(couplings)
        stage(Q, GQ, OQ, 1, correct, correct_ghost, send_s, lambda: g_copy(GS, OS, 0).start())

        @pl.when(turn == STEPS // 2 - 1)
        def _():
            local_part(0)

        @pl.when(turn == STEPS // 2)
        def _():
            wave_part(0)

        return carry

    for copy in tables:
        copy.wait()
    lax.fori_loop(0, STEPS - 1, step, 0)
    predict_stage()
    stage(Q, GQ, OQ, 1, correct, None, lambda: None, None, every=range(1, tiles - 1))
    local_part(1)

    def scaled(z, carry):
        for c in range(3):
            for r in range(inner):
                out[c, z, pl.ds(8 * r, 8), :] = S[c, z + 1, pl.ds(HALO + 8 * r, 8), :] * (1.0 / damping)
        return carry

    lax.fori_loop(0, depth, scaled, 0)
    final = pltpu.make_async_copy(out, end_ref, osem.at[0])
    final.start()
    wave_part(1)
    x_part(0)
    y_part(0)
    last_part(0, mid_out)
    x_part(1)
    y_part(1)
    last_part(1, end_out)
    final.wait()


def phase_table(wave_count, total_length):
    index = np.arange(total_length)[:, None] * np.arange(wave_count)[None, :] % total_length
    phase = index * (2.0 * math.pi / total_length)
    return np.cos(phase), np.sin(phase)


def halves(table):
    big = table.astype(jnp.bfloat16)
    small = (table - big.astype(np.float64)).astype(jnp.bfloat16)
    return big, small


def wave_tables(depth, wide, lanes, nx, ny, nz):
    total_z = depth * nz
    owned = total_z // nx
    x_cos, x_sin = phase_table(KX, wide * nx)
    y_cos, y_sin = phase_table(KY, lanes * ny)
    z_cos, z_sin = phase_table(total_z, total_z)
    big, small = halves(np.concatenate([y_cos, y_sin, -y_sin, y_cos], 1).reshape(ny, lanes, 4 * KY))
    row = np.concatenate([big, small], 2)
    y_all = np.concatenate([row, row], 1)
    big, small = halves(np.concatenate([x_cos, x_sin], 1).reshape(nx, wide, 2 * KX).transpose(0, 2, 1))
    x_all = np.concatenate([big, big, small, small], 2)
    scale = float(wide * nx * lanes * ny * total_z) ** -0.5 / damping
    z_full = np.zeros((nz, nx, 8, nz, 2, depth))
    for first in range(nz):
        for place in range(nz):
            where = (first + place) % nz * depth + np.arange(depth)
            for p, (even, odd) in enumerate(((z_cos, -z_sin), (-z_sin, -z_cos))):
                for part, table in enumerate((even, odd)):
                    values = table[where].T.reshape(nx, owned, depth) * scale
                    z_full[first, :, p * owned : (p + 1) * owned, place, part] = values
    big, small = halves(z_full.reshape(nz, nx * 8, nz * 2 * depth))
    z_all = np.concatenate([big, big, small, small], 2)
    return jnp.asarray(y_all), jnp.asarray(x_all), jnp.asarray(z_all)


def evolve(polar_angle, azimuth, classes, exchange_table):
    depth, wide, lanes = polar_angle.shape
    sizes = nx, ny, nz = (lax.axis_size("gx"), lax.axis_size("gy"), lax.axis_size("gz"))
    owned = depth * nz // nx
    half = KX // nz
    assert nz == 2 and depth * 2 * HALO == lanes and lanes == 4 * KY and 0 < 2 * owned <= 8
    ext = wide + 2 * HALO
    f32, i32, b16 = jnp.float32, jnp.int32, jnp.bfloat16
    hbm = pl.BlockSpec(memory_space=pltpu.HBM)
    anywhere = pl.BlockSpec(memory_space=pl.ANY)
    vmem = pl.BlockSpec(memory_space=pltpu.VMEM)
    V = pltpu.VMEM
    D = pltpu.SemaphoreType.DMA
    modes = jax.ShapeDtypeStruct((owned, 6 * KX * KY), f32)
    return pl.pallas_call(
        functools.partial(evolve_kernel, sizes),
        out_shape=(jax.ShapeDtypeStruct((3, depth, wide, lanes), f32), modes, modes),
        in_specs=[hbm] * 6 + [pl.BlockSpec(memory_space=pltpu.SMEM)],
        out_specs=(anywhere, vmem, vmem),
        scratch_shapes=[
            V((depth, wide, lanes), f32), V((depth, wide, lanes), f32), V((5, depth, wide, lanes), i32),
            V((3, depth + 2, ext, lanes), f32), V((3, depth + 2, ext, lanes), f32),
            V((4, depth + 1, ext, lanes), f32),
            V((3, ext, lanes), f32), V((3, ext, lanes), f32), V((4, ext, lanes), f32),
            V((3, ext, lanes), f32), V((3, ext, lanes), f32), V((ext, lanes), f32),
            V((2, depth, HALO, lanes), f32), V((2, depth, HALO, lanes), f32),
            V((4, depth, HALO, lanes), i32), V((4, depth, HALO, lanes), i32),
            V((5, wide, lanes), f32), V((5, ext, lanes), f32), V((5, ext, lanes), f32),
            V((3, depth, wide, lanes), f32),
            V((2 * lanes, 2 * lanes), b16), V((2 * KX, 4 * wide), b16), V((nx * 8, 8 * nz * depth), b16),
            V((depth * wide, 2 * lanes), b16), V((depth * KX, lanes), f32),
            V((2, nz, 3, 2 * depth, half * KY), f32), V((2, 3, 2 * depth, half * KY), f32),
            V((2, 3, nx, 8, half * KY), f32), V((2, 3, nx - 1, 8, half * KY), f32),
            V((2, 3, ny, 8, half * KY), f32), V((2, 3, nz, 8, half * KY), f32),
            D((8,)), D((8,)), D((6,)), D((6,)), D((4,)), D((4,)), D((3,)), D((3,)), D((1,)), D((8,)),
            D((2, 3)), D((2, 3)), D((2, 3, nx - 1)), D((2, 3, nx - 1)), D((2, 3, ny - 1)), D((2, 3, ny - 1)),
            D((2, 3)), D((2, 3)),
        ],
        compiler_params=pltpu.CompilerParams(collective_id=0, has_side_effects=True, vmem_limit_bytes=60000000),
        name="evolve",
    )(polar_angle, azimuth, classes, *wave_tables(depth, wide, lanes, nx, ny, nz), exchange_table)


def solution(mesh):
    return jax.shard_map(
        evolve,
        mesh=mesh,
        in_specs=(
            P("gz", ("groups", "gx"), "gy"),
            P("gz", ("groups", "gx"), "gy"),
            P(None, "gz", ("groups", "gx"), "gy"),
            P(),
        ),
        out_specs=(
            P(None, "gz", ("groups", "gx"), "gy"),
            P(("groups", "gx"), None),
            P(("groups", "gx"), None),
        ),
        check_vma=False,
    )
```

```python
import functools
import math

import jax
import jax.numpy as jnp
import numpy as np
from jax import lax
from jax.experimental import pallas as pl
from jax.experimental.pallas import tpu as pltpu
from jax.sharding import PartitionSpec as P

KX = 32
KY = 32
STEPS = 4
HALO = 8
MESH = pl.DeviceIdType.MESH

time_step = 0.1
damping = 0.1
HALF_SINE = (0.4999999978578703, -0.02083332246217966, 0.00026040783166918343, -1.5475817235376e-06,
             5.0882140435283864e-09)
HALF_COSINE = (0.9999999997798975, -0.12499999839235146, 0.0026041647630212603, -2.1700563804658615e-05,
               9.671927783275375e-08, -2.5440497387766775e-10)


def horner(coefficients, square):
    total = coefficients[-1]
    for value in coefficients[-2::-1]:
        total = total * square + value
    return total


def sin_cos(angle):
    square = angle * angle
    half_sine = angle * horner(HALF_SINE, square)
    half_cosine = horner(HALF_COSINE, square)
    twice = half_sine + half_sine
    return twice * half_cosine, 1.0 - twice * half_sine


def spins_of(polar, azimuth):
    sine_polar, cosine_polar = sin_cos(polar)
    sine_azimuth, cosine_azimuth = sin_cos(azimuth)
    scaled = sine_polar * damping
    return scaled * cosine_azimuth, scaled * sine_azimuth, cosine_polar * damping


def descent(spin, field):
    s0, s1, s2 = spin
    h0, h1, h2 = field
    w0 = h0 + (s1 * h2 - s2 * h1)
    w1 = h1 + (s2 * h0 - s0 * h2)
    w2 = h2 + (s0 * h1 - s1 * h0)
    return s1 * w2 - s2 * w1, s2 * w0 - s0 * w2, s0 * w1 - s1 * w0


def evolve_kernel(sizes, polar_in, azimuth_in, classes_in, y_in, x_in, z_in, table_ref, end_ref, mid_out, end_out,
                  polar_ref, azimuth_ref, classes_ref, S, Q, J, GS, GQ, GJ, OS, OQ, OJ,
                  low, high, lowk, highk, pack, left_pack, right_pack,
                  y_table, x_table, z_table, along_y, waves_xy, planes, twin_planes, sums, peer_sums, rows_sum, whole,
                  xs, xr, ys, yr, zs, zr, gs, gr, isem, ts, tr, ps, pr, qs, qr, fs, fr):
    nx, ny, nz = sizes
    depth, wide, lanes = polar_ref.shape
    ext = wide + 2 * HALO
    tiles = ext // 8
    inner = wide // 8
    group = 2 * HALO
    me_x, me_y, me_z = lax.axis_index("gx"), lax.axis_index("gy"), lax.axis_index("gz")

    def at(axis, me, n, step):
        return {axis: lax.rem(me + (step + n), n)}

    x_left, x_right = at("gx", me_x, nx, -1), at("gx", me_x, nx, 1)
    y_left, y_right = at("gy", me_y, ny, -1), at("gy", me_y, ny, 1)
    z_down, z_up = at("gz", me_z, nz, -1), at("gz", me_z, nz, 1)
    sides = [y_right] if ny == 2 else [y_right, y_left]

    fetches = [
        pltpu.make_async_copy(polar_in, polar_ref, isem.at[0]),
        pltpu.make_async_copy(azimuth_in, azimuth_ref, isem.at[1]),
        pltpu.make_async_copy(classes_in.at[pl.ds(0, 3)], classes_ref.at[pl.ds(0, 3)], isem.at[2]),
        pltpu.make_async_copy(classes_in.at[4], classes_ref.at[3], isem.at[3]),
        pltpu.make_async_copy(classes_in.at[5, 0], classes_ref.at[4, 0], isem.at[4]),
    ]
    tables = [
        pltpu.make_async_copy(y_in.at[me_y], y_table, isem.at[5]),
        pltpu.make_async_copy(x_in.at[me_x], x_table, isem.at[6]),
        pltpu.make_async_copy(z_in.at[me_z], z_table, isem.at[7]),
    ]
    for copy in fetches + tables:
        copy.start()
    peers_x = [at("gx", me_x, nx, o) for o in range(1, nx)]
    peers_y = [at("gy", me_y, ny, o) for o in range(1, ny)]
    barrier = pltpu.get_barrier_semaphore()
    friends = peers_x + peers_y + [z_up] + [{**x, **y} for x in (x_left, x_right) for y in sides]
    for who in friends:
        pl.semaphore_signal(barrier, inc=1, device_id=who, device_id_type=MESH)
    pl.semaphore_wait(barrier, len(friends))

    def remote(src, dst, send, recv, who):
        return pltpu.make_async_remote_copy(
            src_ref=src, dst_ref=dst, send_sem=send, recv_sem=recv, device_id=who, device_id_type=MESH
        )

    top = pl.ds(wide - HALO, HALO)
    bottom = pl.ds(0, HALO)
    x_copies = []
    for rows, halo, kinds, who in ((top, low, lowk, x_right), (bottom, high, highk, x_left)):
        for src, dst in (
            (polar_in.at[:, rows, :], halo.at[0]),
            (azimuth_in.at[:, rows, :], halo.at[1]),
            (classes_in.at[pl.ds(0, 3), :, rows, :], kinds.at[pl.ds(0, 3)]),
            (classes_in.at[5, 0, rows, :], kinds.at[3, 0]),
        ):
            i = len(x_copies)
            x_copies.append(remote(src, dst, xs.at[i], xr.at[i], who))
    for copy in x_copies:
        copy.start()

    lane = lax.broadcasted_iota(jnp.int32, (8, lanes), 1)
    group_of = lane // group
    place = lane % group
    ratio = time_step / damping
    table = jnp.zeros((8, lanes), jnp.float32)
    for i in range(table_ref.shape[0]):
        table = jnp.where(lane == i, table_ref[i] * ratio, table)

    def lookup(kinds):
        return jnp.take_along_axis(table, kinds, axis=1, mode="promise_in_bounds")

    for f in range(5):
        for r in range(inner):
            pack[f, pl.ds(8 * r, 8), :] = jnp.zeros((8, lanes), jnp.float32)
    for copy in fetches:
        copy.wait()

    def own_first(z, carry):
        mine = group_of == z
        mirror = (group * z + HALO - 1 + lanes - lane) % lanes
        for r in range(inner):
            rows = pl.ds(8 * r, 8)
            values = [polar_ref[z, rows, :], azimuth_ref[z, rows, :]]
            for d in range(3):
                value = lookup(classes_ref[d, z, rows, :])
                J[d, z + 1, pl.ds(HALO + 8 * r, 8), :] = value
                values.append(value)
            for f, value in enumerate(values):
                turned = jnp.take_along_axis(value, mirror, axis=1, mode="promise_in_bounds")
                pack[f, rows, :] = jnp.where(mine, turned, pack[f, rows, :])
        return carry

    lax.fori_loop(0, depth, own_first, 0)

    y_copies = []
    for side, (who, target) in enumerate(zip(sides, (left_pack, right_pack))):
        for part, (src, dst, to) in enumerate((
            (top, pl.ds(0, HALO), {**x_right, **who}),
            (bottom, pl.ds(HALO + wide, HALO), {**x_left, **who}),
            (pl.ds(0, wide), pl.ds(HALO, wide), who),
        )):
            i = 3 * side + part
            y_copies.append(remote(pack.at[:, src, :], target.at[:, dst, :], ys.at[i], yr.at[i], to))
    for copy in y_copies:
        copy.start()

    def own_second(z, carry):
        for r in range(inner):
            rows = pl.ds(8 * r, 8)
            spin = spins_of(polar_ref[z, rows, :], azimuth_ref[z, rows, :])
            for c in range(3):
                S[c, z + 1, pl.ds(HALO + 8 * r, 8), :] = spin[c]
            J[3, z + 1, pl.ds(HALO + 8 * r, 8), :] = lookup(classes_ref[3, z, rows, :])
        return carry

    lax.fori_loop(0, depth, own_second, 0)
    for r in range(inner):
        J[2, 0, pl.ds(HALO + 8 * r, 8), :] = lookup(classes_ref[4, 0, pl.ds(8 * r, 8), :])
    for copy in x_copies:
        copy.wait()

    def edges(z, carry):
        for halo, kinds, row in ((low, lowk, 0), (high, highk, HALO + wide)):
            spin = spins_of(halo[0, z], halo[1, z])
            for c in range(3):
                S[c, z + 1, pl.ds(row, 8), :] = spin[c]
            for d in range(3):
                J[d, z + 1, pl.ds(row, 8), :] = lookup(kinds[d, z])
        return carry

    lax.fori_loop(0, depth, edges, 0)
    J[2, 0, pl.ds(0, 8), :] = lookup(lowk[3, 0])
    J[2, 0, pl.ds(HALO + wide, 8), :] = lookup(highk[3, 0])

    def z_copies(field, base):
        return [
            remote(field.at[:, 1], field.at[:, depth + 1], zs.at[base], zr.at[base], z_down),
            remote(field.at[:, depth], field.at[:, 0], zs.at[base + 1], zr.at[base + 1], z_up),
        ]

    def g_copy(ghost, other, base):
        return remote(ghost, other, gs.at[base], gr.at[base], z_up)

    for copy in z_copies(S, 0):
        copy.start()
    for copy in y_copies:
        copy.wait()
    from_right = left_pack if ny == 2 else right_pack

    def ghosts(r, carry):
        rows = pl.ds(pl.multiple_of(8 * r, 8), 8)
        fields = [jnp.where(place >= HALO, left_pack[f, rows, :], from_right[f, rows, :]) for f in range(5)]
        spin = spins_of(fields[0], fields[1])
        for c in range(3):
            GS[c, rows, :] = spin[c]
        for d in range(3):
            GJ[d, rows, :] = fields[2 + d]
        edge = jnp.zeros((8, lanes), jnp.float32)
        for z in range(depth):
            edge = jnp.where(group_of == z, pltpu.roll(J[1, z + 1, rows, :], group * z + HALO, 1), edge)
        GJ[3, rows, :] = jnp.where(place == HALO - 1, edge, pltpu.roll(fields[3], lanes - 1, 1))
        return carry

    lax.fori_loop(0, tiles, ghosts, 0)
    g_copy(GS, OS, 0).start()
    g_copy(GJ.at[2], OJ, 2).start()

    def corners(z, carry):
        for row in (0, HALO + wide):
            rows = pl.ds(row, 8)
            outside = pltpu.roll(GJ[1, rows, :], lanes - (group * z + HALO), 1)
            J[3, z + 1, rows, :] = jnp.where(lane == 0, outside, pltpu.roll(J[1, z + 1, rows, :], 1, 1))
        return carry

    lax.fori_loop(0, depth, corners, 0)

    def x_pair(ref, r, value):
        ahead = ref[pl.ds(8 * r + 1, 8), :] if r < tiles - 1 else pltpu.roll(value, 7, 0)
        behind = ref[pl.ds(8 * r - 1, 8), :] if r > 0 else pltpu.roll(value, 1, 0)
        return ahead, behind

    def plane(F, G, z, finish, rows_of):
        up_shift = lanes - (group * z + HALO)
        for r in rows_of:
            rows = pl.ds(8 * r, 8)
            c0, c1, c2, c4 = (J[d, z + 1, rows, :] for d in range(4))
            c3 = J[0, z + 1, pl.ds(8 * r - 1, 8), :] if r > 0 else pltpu.roll(c0, 1, 0)
            c5 = J[2, z, rows, :]
            spin, field = [], []
            for c in range(3):
                M = F[c, z + 1, rows, :]
                ahead, behind = x_pair(F.at[c, z + 1], r, M)
                U = pltpu.roll(G[c, rows, :], up_shift, 1)
                right = jnp.where(lane == lanes - 1, U, pltpu.roll(M, lanes - 1, 1))
                left = jnp.where(lane == 0, U, pltpu.roll(M, 1, 1))
                total = (c0 * ahead + c3 * behind) + (c2 * F[c, z + 2, rows, :] + c5 * F[c, z, rows, :])
                total = total + (c1 * right + c4 * left)
                spin.append(M)
                field.append(total)
            finish(spin, descent(spin, field), z, rows)

    def ghost_pass(F, G, other, finish):
        for r in range(tiles):
            rows = pl.ds(8 * r, 8)
            c0, c1, c2, c4 = (GJ[d, rows, :] for d in range(4))
            c3 = GJ[0, pl.ds(8 * r - 1, 8), :] if r > 0 else pltpu.roll(c0, 1, 0)
            c5 = pltpu.roll(jnp.where(lane < lanes - group, c2, OJ[rows, :]), group, 1)
            spin, field = [], []
            for c in range(3):
                M = G[c, rows, :]
                O = other[c, rows, :]
                I = M
                for z in range(depth):
                    I = jnp.where(group_of == z, pltpu.roll(F[c, z + 1, rows, :], group * z + HALO, 1), I)
                ahead, behind = x_pair(G.at[c], r, M)
                right = jnp.where(place == HALO, I, pltpu.roll(M, 1, 1))
                left = jnp.where(place == HALO - 1, I, pltpu.roll(M, lanes - 1, 1))
                above = pltpu.roll(jnp.where(lane >= group, M, O), lanes - group, 1)
                below = pltpu.roll(jnp.where(lane < lanes - group, M, O), group, 1)
                total = (c0 * ahead + c3 * behind) + (c2 * above + c5 * below)
                total = total + (c1 * right + c4 * left)
                spin.append(M)
                field.append(total)
            finish(spin, descent(spin, field), rows)

    def predict(spin, change, z, rows):
        for c in range(3):
            Q[c, z + 1, rows, :] = spin[c] - change[c]

    def predict_ghost(spin, change, rows):
        for c in range(3):
            GQ[c, rows, :] = spin[c] - change[c]

    def correct(spin, change, z, rows):
        for c in range(3):
            S[c, z + 1, rows, :] = 0.5 * (S[c, z + 1, rows, :] + (spin[c] - change[c]))

    def correct_ghost(spin, change, rows):
        for c in range(3):
            GS[c, rows, :] = 0.5 * (GS[c, rows, :] + (spin[c] - change[c]))

    def stage(F, G, O, base, finish, finish_ghost, send_main, send_ghost, first=None, every=range(tiles)):
        def inside(i, carry):
            plane(F, G, 2 * i + 1, finish, every)
            plane(F, G, 2 * i + 2, finish, every)
            return carry

        lax.fori_loop(0, (depth - 2) // 2, inside, 0)
        for copy in z_copies(F, 2 * base):
            copy.wait()
        plane(F, G, 0, finish, every)
        plane(F, G, depth - 1, finish, every)
        send_main()
        g_copy(G, O, base).wait()
        if finish_ghost is None:
            return
        if first is not None:
            first()
        ghost_pass(F, G, O, finish_ghost)
        send_ghost()

    def split(value):
        big = value.astype(jnp.bfloat16)
        return big, (value - big.astype(jnp.float32)).astype(jnp.bfloat16)

    def dot(a, b):
        return jnp.dot(a, b, preferred_element_type=jnp.float32)

    half = KX // nz
    quad = lanes // KY

    def transform(f, c):
        for z in range(depth):
            big, small = split(S[c, z + 1, pl.ds(HALO, wide), :])
            along_y[pl.ds(z * wide, wide), pl.ds(0, lanes)] = big
            along_y[pl.ds(z * wide, wide), pl.ds(lanes, lanes)] = small
        both = dot(along_y[...], y_table[...])
        both = both[:, :lanes] + both[:, lanes:]
        for z in range(0, depth, 2):
            parts = []
            for i in (z, z + 1):
                big, small = split(both[i * wide : (i + 1) * wide])
                parts.append(jnp.concatenate([big, small, big, small], 0))
            along_x = dot(x_table[...], jnp.concatenate(parts, 1))
            for i in range(2):
                mine = along_x[:, i * lanes : (i + 1) * lanes]
                waves_xy[pl.ds((z + i) * KX, KX), :] = mine[:KX] + pltpu.roll(mine[KX:], lanes // 2, 1)
        slot = lane // KY
        for h in range(nz):
            for j in range(half // quad):
                loads = [waves_xy[pl.ds(h * half + j * quad + k, depth, stride=KX), :] for k in range(quad)]
                for p in range(2):
                    total = None
                    for k, value in enumerate(loads):
                        turn = (k - p) % quad * KY
                        value = pltpu.roll(value, turn, 1) if turn else value
                        total = value if total is None else jnp.where(slot == k, value, total)
                    planes[f, h, c, pl.ds(p * depth, depth), pl.ds(j * lanes, lanes)] = total

    def swap(f, c):
        return remote(planes.at[f, 1 - me_z, c], twin_planes.at[f, c], ts.at[f, c], tr.at[f, c], z_up)

    def waves(f, c):
        stacked = jnp.concatenate([planes[f, me_z, c], twin_planes[f, c]], 0)
        big, small = split(stacked)
        result = dot(z_table[...], jnp.concatenate([big, small, big, small], 0))
        for b in range(nx):
            sums[f, c, b] = result[8 * b : 8 * b + 8]

    def x_sends(f, c):
        return [
            remote(sums.at[f, c, lax.rem(me_x + o, nx)], peer_sums.at[f, c, o - 1], ps.at[f, c, o - 1],
                   pr.at[f, c, o - 1], peers_x[o - 1])
            for o in range(1, nx)
        ]

    def y_sends(f, c):
        return [
            remote(rows_sum.at[f, c, me_y], rows_sum.at[f, c, me_y], qs.at[f, c, o - 1], qr.at[f, c, o - 1],
                   peers_y[o - 1])
            for o in range(1, ny)
        ]

    def share(f, c):
        return remote(whole.at[f, c, me_z], whole.at[f, c, me_z], fs.at[f, c], fr.at[f, c], z_up)

    def local_part(f):
        for c in range(3):
            transform(f, c)
            swap(f, c).start()

    def wave_part(f):
        for c in range(3):
            swap(f, c).wait()
            waves(f, c)
            for copy in reversed(x_sends(f, c)):
                copy.start()

    def x_part(f):
        for c in range(3):
            for copy in x_sends(f, c):
                copy.wait()
            total = sums[f, c, me_x]
            for o in range(1, nx):
                total = total + peer_sums[f, c, o - 1]
            rows_sum[f, c, me_y] = total
            for copy in y_sends(f, c):
                copy.start()

    def y_part(f):
        for c in range(3):
            for copy in y_sends(f, c):
                copy.wait()
            total = rows_sum[f, c, 0]
            for o in range(1, ny):
                total = total + rows_sum[f, c, o]
            whole[f, c, me_z] = total
            share(f, c).start()

    def last_part(f, target):
        owned = target.shape[0]
        for c in range(3):
            share(f, c).wait()
            for h in range(nz):
                for p in range(2):
                    start = (p * 3 + c) * KX * KY + h * half * KY
                    target[:, pl.ds(start, half * KY)] = whole[f, c, h, pl.ds(p * owned, owned), :]

    def send_q():
        for copy in z_copies(Q, 2):
            copy.start()

    def send_s():
        for copy in z_copies(S, 0):
            copy.start()

    def predict_stage(first=None):
        stage(S, GS, OS, 0, predict, predict_ghost, send_q, lambda: g_copy(GQ, OQ, 1).start(), first)

    def step(turn, carry):
        def couplings():
            @pl.when(turn == 0)
            def _():
                g_copy(GJ.at[2], OJ, 2).wait()

        predict_stage(couplings)
        stage(Q, GQ, OQ, 1, correct, correct_ghost, send_s, lambda: g_copy(GS, OS, 0).start())

        @pl.when(turn == STEPS // 2 - 1)
        def _():
            local_part(0)

        @pl.when(turn == STEPS // 2)
        def _():
            wave_part(0)

        return carry

    for copy in tables:
        copy.wait()
    lax.fori_loop(0, STEPS - 1, step, 0)
    predict_stage()
    stage(Q, GQ, OQ, 1, correct, None, lambda: None, None, every=range(1, tiles - 1))
    local_part(1)

    def scaled(z, carry):
        for c in range(3):
            for r in range(inner):
                end_ref[c, z, pl.ds(8 * r, 8), :] = S[c, z + 1, pl.ds(HALO + 8 * r, 8), :] * (1.0 / damping)
        return carry

    lax.fori_loop(0, depth, scaled, 0)
    wave_part(1)
    x_part(0)
    y_part(0)
    last_part(0, mid_out)
    x_part(1)
    y_part(1)
    last_part(1, end_out)


def write_kernel(*refs):
    count = (len(refs) - 1) // 2
    copies = [pltpu.make_async_copy(refs[i], refs[count + i], refs[-1].at[i]) for i in range(count)]
    for copy in copies:
        copy.start()
    for copy in copies:
        copy.wait()


def phase_table(wave_count, total_length):
    index = np.arange(total_length)[:, None] * np.arange(wave_count)[None, :] % total_length
    phase = index * (2.0 * math.pi / total_length)
    return np.cos(phase), np.sin(phase)


def halves(table):
    big = table.astype(jnp.bfloat16)
    small = (table - big.astype(np.float64)).astype(jnp.bfloat16)
    return big, small


def wave_tables(depth, wide, lanes, nx, ny, nz):
    total_z = depth * nz
    owned = total_z // nx
    x_cos, x_sin = phase_table(KX, wide * nx)
    y_cos, y_sin = phase_table(KY, lanes * ny)
    z_cos, z_sin = phase_table(total_z, total_z)
    big, small = halves(np.concatenate([y_cos, y_sin, -y_sin, y_cos], 1).reshape(ny, lanes, 4 * KY))
    row = np.concatenate([big, small], 2)
    y_all = np.concatenate([row, row], 1)
    big, small = halves(np.concatenate([x_cos, x_sin], 1).reshape(nx, wide, 2 * KX).transpose(0, 2, 1))
    x_all = np.concatenate([big, big, small, small], 2)
    scale = float(wide * nx * lanes * ny * total_z) ** -0.5 / damping
    z_full = np.zeros((nz, nx, 8, nz, 2, depth))
    for first in range(nz):
        for place in range(nz):
            where = (first + place) % nz * depth + np.arange(depth)
            for p, (even, odd) in enumerate(((z_cos, -z_sin), (-z_sin, -z_cos))):
                for part, table in enumerate((even, odd)):
                    values = table[where].T.reshape(nx, owned, depth) * scale
                    z_full[first, :, p * owned : (p + 1) * owned, place, part] = values
    big, small = halves(z_full.reshape(nz, nx * 8, nz * 2 * depth))
    z_all = np.concatenate([big, big, small, small], 2)
    return jnp.asarray(y_all), jnp.asarray(x_all), jnp.asarray(z_all)


def evolve(polar_angle, azimuth, classes, exchange_table):
    depth, wide, lanes = polar_angle.shape
    sizes = nx, ny, nz = (lax.axis_size("gx"), lax.axis_size("gy"), lax.axis_size("gz"))
    owned = depth * nz // nx
    half = KX // nz
    assert nz == 2 and depth * 2 * HALO == lanes and lanes == 4 * KY and 0 < 2 * owned <= 8
    ext = wide + 2 * HALO
    f32, i32, b16 = jnp.float32, jnp.int32, jnp.bfloat16
    hbm = pl.BlockSpec(memory_space=pltpu.HBM)
    anywhere = pl.BlockSpec(memory_space=pl.ANY)
    vmem = pl.BlockSpec(memory_space=pltpu.VMEM)
    V = pltpu.VMEM
    D = pltpu.SemaphoreType.DMA
    modes = jax.ShapeDtypeStruct((owned, 6 * KX * KY), f32)
    shapes = (jax.ShapeDtypeStruct((3, depth, wide, lanes), f32), modes, modes)
    results = pl.pallas_call(
        functools.partial(evolve_kernel, sizes),
        out_shape=shapes,
        in_specs=[hbm] * 6 + [pl.BlockSpec(memory_space=pltpu.SMEM)],
        out_specs=(vmem, vmem, vmem),
        scratch_shapes=[
            V((depth, wide, lanes), f32), V((depth, wide, lanes), f32), V((5, depth, wide, lanes), i32),
            V((3, depth + 2, ext, lanes), f32), V((3, depth + 2, ext, lanes), f32),
            V((4, depth + 1, ext, lanes), f32),
            V((3, ext, lanes), f32), V((3, ext, lanes), f32), V((4, ext, lanes), f32),
            V((3, ext, lanes), f32), V((3, ext, lanes), f32), V((ext, lanes), f32),
            V((2, depth, HALO, lanes), f32), V((2, depth, HALO, lanes), f32),
            V((4, depth, HALO, lanes), i32), V((4, depth, HALO, lanes), i32),
            V((5, wide, lanes), f32), V((5, ext, lanes), f32), V((5, ext, lanes), f32),
            V((2 * lanes, 2 * lanes), b16), V((2 * KX, 4 * wide), b16), V((nx * 8, 8 * nz * depth), b16),
            V((depth * wide, 2 * lanes), b16), V((depth * KX, lanes), f32),
            V((2, nz, 3, 2 * depth, half * KY), f32), V((2, 3, 2 * depth, half * KY), f32),
            V((2, 3, nx, 8, half * KY), f32), V((2, 3, nx - 1, 8, half * KY), f32),
            V((2, 3, ny, 8, half * KY), f32), V((2, 3, nz, 8, half * KY), f32),
            D((8,)), D((8,)), D((6,)), D((6,)), D((4,)), D((4,)), D((3,)), D((3,)), D((8,)),
            D((2, 3)), D((2, 3)), D((2, 3, nx - 1)), D((2, 3, nx - 1)), D((2, 3, ny - 1)), D((2, 3, ny - 1)),
            D((2, 3)), D((2, 3)),
        ],
        compiler_params=pltpu.CompilerParams(collective_id=0, has_side_effects=True, vmem_limit_bytes=60000000),
        name="evolve",
    )(polar_angle, azimuth, classes, *wave_tables(depth, wide, lanes, nx, ny, nz), exchange_table)
    return pl.pallas_call(
        write_kernel,
        out_shape=shapes,
        in_specs=[vmem] * 3,
        out_specs=(anywhere,) * 3,
        scratch_shapes=[D((3,))],
        name="write",
    )(*results)


def solution(mesh):
    return jax.shard_map(
        evolve,
        mesh=mesh,
        in_specs=(
            P("gz", ("groups", "gx"), "gy"),
            P("gz", ("groups", "gx"), "gy"),
            P(None, "gz", ("groups", "gx"), "gy"),
            P(),
        ),
        out_specs=(
            P(None, "gz", ("groups", "gx"), "gy"),
            P(("groups", "gx"), None),
            P(("groups", "gx"), None),
        ),
        check_vma=False,
    )
```

```python
import functools
import math

import jax
import jax.numpy as jnp
import numpy as np
from jax import lax
from jax.experimental import pallas as pl
from jax.experimental.pallas import tpu as pltpu
from jax.sharding import PartitionSpec as P

KX = 32
KY = 32
STEPS = 4
HALO = 8
MESH = pl.DeviceIdType.MESH

time_step = 0.1
damping = 0.1
HALF_SINE = (0.4999999978578703, -0.02083332246217966, 0.00026040783166918343, -1.5475817235376e-06,
             5.0882140435283864e-09)
HALF_COSINE = (0.9999999997798975, -0.12499999839235146, 0.0026041647630212603, -2.1700563804658615e-05,
               9.671927783275375e-08, -2.5440497387766775e-10)


def horner(coefficients, square):
    total = coefficients[-1]
    for value in coefficients[-2::-1]:
        total = total * square + value
    return total


def sin_cos(angle):
    square = angle * angle
    half_sine = angle * horner(HALF_SINE, square)
    half_cosine = horner(HALF_COSINE, square)
    twice = half_sine + half_sine
    return twice * half_cosine, 1.0 - twice * half_sine


def spins_of(polar, azimuth):
    sine_polar, cosine_polar = sin_cos(polar)
    sine_azimuth, cosine_azimuth = sin_cos(azimuth)
    scaled = sine_polar * damping
    return scaled * cosine_azimuth, scaled * sine_azimuth, cosine_polar * damping


def descent(spin, field):
    s0, s1, s2 = spin
    h0, h1, h2 = field
    w0 = h0 + (s1 * h2 - s2 * h1)
    w1 = h1 + (s2 * h0 - s0 * h2)
    w2 = h2 + (s0 * h1 - s1 * h0)
    return s1 * w2 - s2 * w1, s2 * w0 - s0 * w2, s0 * w1 - s1 * w0


def evolve_kernel(sizes, polar_in, azimuth_in, classes_in, y_in, x_in, z_in, spread_in, table_ref, end_ref, mid_out, end_out,
                  polar_ref, azimuth_ref, classes_ref, S, Q, J, GS, GQ, GJ, OS, OQ, OJ,
                  low, high, lowk, highk, pack, left_pack, right_pack,
                  US, UQ, ins, spread_table, y_table, x_table, z_table, along_y, waves_xy, planes, twin_planes, sums, peer_sums, rows_sum, whole,
                  xs, xr, ys, yr, zs, zr, gs, gr, isem, ts, tr, ps, pr, qs, qr, fs, fr):
    nx, ny, nz = sizes
    depth, wide, lanes = polar_ref.shape
    ext = wide + 2 * HALO
    tiles = ext // 8
    inner = wide // 8
    group = 2 * HALO
    me_x, me_y, me_z = lax.axis_index("gx"), lax.axis_index("gy"), lax.axis_index("gz")

    def at(axis, me, n, step):
        return {axis: lax.rem(me + (step + n), n)}

    x_left, x_right = at("gx", me_x, nx, -1), at("gx", me_x, nx, 1)
    y_left, y_right = at("gy", me_y, ny, -1), at("gy", me_y, ny, 1)
    z_down, z_up = at("gz", me_z, nz, -1), at("gz", me_z, nz, 1)
    sides = [y_right] if ny == 2 else [y_right, y_left]

    fetches = [
        pltpu.make_async_copy(polar_in, polar_ref, isem.at[0]),
        pltpu.make_async_copy(azimuth_in, azimuth_ref, isem.at[1]),
        pltpu.make_async_copy(classes_in.at[pl.ds(0, 3)], classes_ref.at[pl.ds(0, 3)], isem.at[2]),
        pltpu.make_async_copy(classes_in.at[4], classes_ref.at[3], isem.at[3]),
        pltpu.make_async_copy(classes_in.at[5, 0], classes_ref.at[4, 0], isem.at[4]),
    ]
    tables = [
        pltpu.make_async_copy(y_in.at[me_y], y_table, isem.at[5]),
        pltpu.make_async_copy(x_in.at[me_x], x_table, isem.at[6]),
        pltpu.make_async_copy(z_in.at[me_z], z_table, isem.at[7]),
        pltpu.make_async_copy(spread_in, spread_table, isem.at[8]),
    ]
    for copy in fetches + tables:
        copy.start()
    peers_x = [at("gx", me_x, nx, o) for o in range(1, nx)]
    peers_y = [at("gy", me_y, ny, o) for o in range(1, ny)]
    barrier = pltpu.get_barrier_semaphore()
    friends = peers_x + peers_y + [z_up] + [{**x, **y} for x in (x_left, x_right) for y in sides]
    for who in friends:
        pl.semaphore_signal(barrier, inc=1, device_id=who, device_id_type=MESH)
    pl.semaphore_wait(barrier, len(friends))

    def remote(src, dst, send, recv, who):
        return pltpu.make_async_remote_copy(
            src_ref=src, dst_ref=dst, send_sem=send, recv_sem=recv, device_id=who, device_id_type=MESH
        )

    def split(value):
        big = value.astype(jnp.bfloat16)
        return big, (value - big.astype(jnp.float32)).astype(jnp.bfloat16)

    def dot(a, b):
        return jnp.dot(a, b, preferred_element_type=jnp.float32)

    top = pl.ds(wide - HALO, HALO)
    bottom = pl.ds(0, HALO)
    x_copies = []
    for rows, halo, kinds, who in ((top, low, lowk, x_right), (bottom, high, highk, x_left)):
        for src, dst in (
            (polar_in.at[:, rows, :], halo.at[0]),
            (azimuth_in.at[:, rows, :], halo.at[1]),
            (classes_in.at[pl.ds(0, 3), :, rows, :], kinds.at[pl.ds(0, 3)]),
            (classes_in.at[5, 0, rows, :], kinds.at[3, 0]),
        ):
            i = len(x_copies)
            x_copies.append(remote(src, dst, xs.at[i], xr.at[i], who))
    for copy in x_copies:
        copy.start()

    lane = lax.broadcasted_iota(jnp.int32, (8, lanes), 1)
    group_of = lane // group
    place = lane % group
    ratio = time_step / damping
    table = jnp.zeros((8, lanes), jnp.float32)
    for i in range(table_ref.shape[0]):
        table = jnp.where(lane == i, table_ref[i] * ratio, table)

    def lookup(kinds):
        return jnp.take_along_axis(table, kinds, axis=1, mode="promise_in_bounds")

    for f in range(5):
        for r in range(inner):
            pack[f, pl.ds(8 * r, 8), :] = jnp.zeros((8, lanes), jnp.float32)
    for copy in fetches:
        copy.wait()

    def own_first(z, carry):
        mine = group_of == z
        mirror = (group * z + HALO - 1 + lanes - lane) % lanes
        for r in range(inner):
            rows = pl.ds(8 * r, 8)
            values = [polar_ref[z, rows, :], azimuth_ref[z, rows, :]]
            for d in range(3):
                value = lookup(classes_ref[d, z, rows, :])
                J[d, z + 1, pl.ds(HALO + 8 * r, 8), :] = value
                values.append(value)
            for f, value in enumerate(values):
                turned = jnp.take_along_axis(value, mirror, axis=1, mode="promise_in_bounds")
                pack[f, rows, :] = jnp.where(mine, turned, pack[f, rows, :])
        return carry

    lax.fori_loop(0, depth, own_first, 0)

    y_copies = []
    for side, (who, target) in enumerate(zip(sides, (left_pack, right_pack))):
        for part, (src, dst, to) in enumerate((
            (top, pl.ds(0, HALO), {**x_right, **who}),
            (bottom, pl.ds(HALO + wide, HALO), {**x_left, **who}),
            (pl.ds(0, wide), pl.ds(HALO, wide), who),
        )):
            i = 3 * side + part
            y_copies.append(remote(pack.at[:, src, :], target.at[:, dst, :], ys.at[i], yr.at[i], to))
    for copy in y_copies:
        copy.start()

    def own_second(z, carry):
        for r in range(inner):
            rows = pl.ds(8 * r, 8)
            spin = spins_of(polar_ref[z, rows, :], azimuth_ref[z, rows, :])
            for c in range(3):
                S[c, z + 1, pl.ds(HALO + 8 * r, 8), :] = spin[c]
            J[3, z + 1, pl.ds(HALO + 8 * r, 8), :] = lookup(classes_ref[3, z, rows, :])
        return carry

    lax.fori_loop(0, depth, own_second, 0)
    for r in range(inner):
        J[2, 0, pl.ds(HALO + 8 * r, 8), :] = lookup(classes_ref[4, 0, pl.ds(8 * r, 8), :])
    for copy in x_copies:
        copy.wait()

    def edges(z, carry):
        for halo, kinds, row in ((low, lowk, 0), (high, highk, HALO + wide)):
            spin = spins_of(halo[0, z], halo[1, z])
            for c in range(3):
                S[c, z + 1, pl.ds(row, 8), :] = spin[c]
            for d in range(3):
                J[d, z + 1, pl.ds(row, 8), :] = lookup(kinds[d, z])
        return carry

    lax.fori_loop(0, depth, edges, 0)
    J[2, 0, pl.ds(0, 8), :] = lookup(lowk[3, 0])
    J[2, 0, pl.ds(HALO + wide, 8), :] = lookup(highk[3, 0])

    def z_copies(field, base):
        return [
            remote(field.at[:, 1], field.at[:, depth + 1], zs.at[base], zr.at[base], z_down),
            remote(field.at[:, depth], field.at[:, 0], zs.at[base + 1], zr.at[base + 1], z_up),
        ]

    def spread(G, U):
        big, small = split(G[...].reshape(3 * ext, lanes))
        both = jnp.concatenate([big, small], 1)
        for k in range(depth // 2):
            cols = pl.ds(2 * lanes * k, 2 * lanes)
            U[:, :, cols] = dot(both, spread_table[:, cols]).reshape(3, ext, 2 * lanes)

    def g_copy(ghost, other, base):
        return remote(ghost, other, gs.at[base], gr.at[base], z_up)

    for copy in z_copies(S, 0):
        copy.start()
    for copy in y_copies:
        copy.wait()
    from_right = left_pack if ny == 2 else right_pack

    def ghosts(r, carry):
        rows = pl.ds(pl.multiple_of(8 * r, 8), 8)
        fields = [jnp.where(place >= HALO, left_pack[f, rows, :], from_right[f, rows, :]) for f in range(5)]
        spin = spins_of(fields[0], fields[1])
        for c in range(3):
            GS[c, rows, :] = spin[c]
        for d in range(3):
            GJ[d, rows, :] = fields[2 + d]
        edge = jnp.zeros((8, lanes), jnp.float32)
        for z in range(depth):
            edge = jnp.where(group_of == z, pltpu.roll(J[1, z + 1, rows, :], group * z + HALO, 1), edge)
        GJ[3, rows, :] = jnp.where(place == HALO - 1, edge, pltpu.roll(fields[3], lanes - 1, 1))
        return carry

    lax.fori_loop(0, tiles, ghosts, 0)
    g_copy(GS, OS, 0).start()
    g_copy(GJ.at[2], OJ, 2).start()
    for copy in tables:
        copy.wait()
    spread(GS, US)

    def corners(z, carry):
        for row in (0, HALO + wide):
            rows = pl.ds(row, 8)
            outside = pltpu.roll(GJ[1, rows, :], lanes - (group * z + HALO), 1)
            J[3, z + 1, rows, :] = jnp.where(lane == 0, outside, pltpu.roll(J[1, z + 1, rows, :], 1, 1))
        return carry

    lax.fori_loop(0, depth, corners, 0)

    def x_pair(ref, r, value):
        ahead = ref[pl.ds(8 * r + 1, 8), :] if r < tiles - 1 else pltpu.roll(value, 7, 0)
        behind = ref[pl.ds(8 * r - 1, 8), :] if r > 0 else pltpu.roll(value, 1, 0)
        return ahead, behind

    def plane_tile(F, U_ref, z, finish, r):
        rows = pl.ds(8 * r, 8)
        c0, c1, c2, c4 = (J[d, z + 1, rows, :] for d in range(4))
        c3 = J[0, z + 1, pl.ds(8 * r - 1, 8), :] if r > 0 else pltpu.roll(c0, 1, 0)
        c5 = J[2, z, rows, :]
        spin, field = [], []
        for c in range(3):
            M = F[c, z + 1, rows, :]
            ahead, behind = x_pair(F.at[c, z + 1], r, M)
            U = U_ref[c, rows, pl.ds(z * lanes, lanes)]
            right = jnp.where(lane == lanes - 1, U, pltpu.roll(M, lanes - 1, 1))
            left = jnp.where(lane == 0, U, pltpu.roll(M, 1, 1))
            total = (c0 * ahead + c3 * behind) + (c2 * F[c, z + 2, rows, :] + c5 * F[c, z, rows, :])
            total = total + (c1 * right + c4 * left)
            spin.append(M)
            field.append(total)
        finish(spin, descent(spin, field), z, rows)

    def collect(F, r):
        rows = pl.ds(8 * r, 8)
        for c in range(3):
            I = pltpu.roll(F[c, 1, rows, :], HALO, 1)
            for z in range(1, depth):
                I = jnp.where(group_of == z, pltpu.roll(F[c, z + 1, rows, :], group * z + HALO, 1), I)
            ins[c, rows, :] = I

    def ghost_tile(G, other, finish, r):
        rows = pl.ds(8 * r, 8)
        c0, c1, c2, c4 = (GJ[d, rows, :] for d in range(4))
        c3 = GJ[0, pl.ds(8 * r - 1, 8), :] if r > 0 else pltpu.roll(c0, 1, 0)
        c5 = pltpu.roll(jnp.where(lane < lanes - group, c2, OJ[rows, :]), group, 1)
        spin, field = [], []
        for c in range(3):
            M = G[c, rows, :]
            O = other[c, rows, :]
            I = ins[c, rows, :]
            ahead, behind = x_pair(G.at[c], r, M)
            right = jnp.where(place == HALO, I, pltpu.roll(M, 1, 1))
            left = jnp.where(place == HALO - 1, I, pltpu.roll(M, lanes - 1, 1))
            above = pltpu.roll(jnp.where(lane >= group, M, O), lanes - group, 1)
            below = pltpu.roll(jnp.where(lane < lanes - group, M, O), group, 1)
            total = (c0 * ahead + c3 * behind) + (c2 * above + c5 * below)
            total = total + (c1 * right + c4 * left)
            spin.append(M)
            field.append(total)
        finish(spin, descent(spin, field), rows)

    def predict(spin, change, z, rows):
        for c in range(3):
            Q[c, z + 1, rows, :] = spin[c] - change[c]

    def predict_ghost(spin, change, rows):
        for c in range(3):
            GQ[c, rows, :] = spin[c] - change[c]

    def correct(spin, change, z, rows):
        for c in range(3):
            S[c, z + 1, rows, :] = 0.5 * (S[c, z + 1, rows, :] + (spin[c] - change[c]))

    def correct_ghost(spin, change, rows):
        for c in range(3):
            GS[c, rows, :] = 0.5 * (GS[c, rows, :] + (spin[c] - change[c]))

    def stage(F, G, O, U, base, finish, finish_ghost, send_main, send_ghost, first=None, every=range(tiles)):
        for r in every:
            if finish_ghost is not None:
                collect(F, r)
            for z in range(1, depth - 1):
                plane_tile(F, U, z, finish, r)
        for copy in z_copies(F, 2 * base):
            copy.wait()
        for r in every:
            for z in (0, depth - 1):
                plane_tile(F, U, z, finish, r)
        send_main()
        g_copy(G, O, base).wait()
        if first is not None:
            first()
        if finish_ghost is not None:
            for r in every:
                ghost_tile(G, O, finish_ghost, r)
            send_ghost()

    half = KX // nz
    quad = lanes // KY

    def transform(f, c):
        for z in range(depth):
            big, small = split(S[c, z + 1, pl.ds(HALO, wide), :])
            along_y[pl.ds(z * wide, wide), pl.ds(0, lanes)] = big
            along_y[pl.ds(z * wide, wide), pl.ds(lanes, lanes)] = small
        both = dot(along_y[...], y_table[...])
        both = both[:, :lanes] + both[:, lanes:]
        for z in range(0, depth, 2):
            parts = []
            for i in (z, z + 1):
                big, small = split(both[i * wide : (i + 1) * wide])
                parts.append(jnp.concatenate([big, small, big, small], 0))
            along_x = dot(x_table[...], jnp.concatenate(parts, 1))
            for i in range(2):
                mine = along_x[:, i * lanes : (i + 1) * lanes]
                waves_xy[pl.ds((z + i) * KX, KX), :] = mine[:KX] + pltpu.roll(mine[KX:], lanes // 2, 1)
        slot = lane // KY
        for h in range(nz):
            for j in range(half // quad):
                loads = [waves_xy[pl.ds(h * half + j * quad + k, depth, stride=KX), :] for k in range(quad)]
                for p in range(2):
                    total = None
                    for k, value in enumerate(loads):
                        turn = (k - p) % quad * KY
                        value = pltpu.roll(value, turn, 1) if turn else value
                        total = value if total is None else jnp.where(slot == k, value, total)
                    planes[f, h, c, pl.ds(p * depth, depth), pl.ds(j * lanes, lanes)] = total

    def swap(f, c):
        return remote(planes.at[f, 1 - me_z, c], twin_planes.at[f, c], ts.at[f, c], tr.at[f, c], z_up)

    def waves(f, c):
        stacked = jnp.concatenate([planes[f, me_z, c], twin_planes[f, c]], 0)
        big, small = split(stacked)
        result = dot(z_table[...], jnp.concatenate([big, small, big, small], 0))
        for b in range(nx):
            sums[f, c, b] = result[8 * b : 8 * b + 8]

    def x_sends(f, c):
        return [
            remote(sums.at[f, c, lax.rem(me_x + o, nx)], peer_sums.at[f, c, o - 1], ps.at[f, c, o - 1],
                   pr.at[f, c, o - 1], peers_x[o - 1])
            for o in range(1, nx)
        ]

    def y_sends(f, c):
        return [
            remote(rows_sum.at[f, c, me_y], rows_sum.at[f, c, me_y], qs.at[f, c, o - 1], qr.at[f, c, o - 1],
                   peers_y[o - 1])
            for o in range(1, ny)
        ]

    def share(f, c):
        return remote(whole.at[f, c, me_z], whole.at[f, c, me_z], fs.at[f, c], fr.at[f, c], z_up)

    def local_part(f):
        for c in range(3):
            transform(f, c)
            swap(f, c).start()

    def wave_part(f):
        for c in range(3):
            swap(f, c).wait()
            waves(f, c)
            for copy in reversed(x_sends(f, c)):
                copy.start()

    def x_part(f):
        for c in range(3):
            for copy in x_sends(f, c):
                copy.wait()
            total = sums[f, c, me_x]
            for o in range(1, nx):
                total = total + peer_sums[f, c, o - 1]
            rows_sum[f, c, me_y] = total
            for copy in y_sends(f, c):
                copy.start()

    def y_part(f):
        for c in range(3):
            for copy in y_sends(f, c):
                copy.wait()
            total = rows_sum[f, c, 0]
            for o in range(1, ny):
                total = total + rows_sum[f, c, o]
            whole[f, c, me_z] = total
            share(f, c).start()

    def last_part(f, target):
        owned = target.shape[0]
        for c in range(3):
            share(f, c).wait()
            for h in range(nz):
                for p in range(2):
                    start = (p * 3 + c) * KX * KY + h * half * KY
                    target[:, pl.ds(start, half * KY)] = whole[f, c, h, pl.ds(p * owned, owned), :]

    def send_q():
        for copy in z_copies(Q, 2):
            copy.start()

    def send_s():
        for copy in z_copies(S, 0):
            copy.start()

    def predict_stage(first=None):
        def send_ghost():
            g_copy(GQ, OQ, 1).start()
            spread(GQ, UQ)

        stage(S, GS, OS, US, 0, predict, predict_ghost, send_q, send_ghost, first)

    def step(turn, carry):
        def couplings():
            @pl.when(turn == 0)
            def _():
                g_copy(GJ.at[2], OJ, 2).wait()

        def send_ghost():
            g_copy(GS, OS, 0).start()
            spread(GS, US)

        predict_stage(couplings)
        stage(Q, GQ, OQ, UQ, 1, correct, correct_ghost, send_s, send_ghost)

        @pl.when(turn == STEPS // 2 - 1)
        def _():
            local_part(0)

        @pl.when(turn == STEPS // 2)
        def _():
            wave_part(0)

        return carry

    lax.fori_loop(0, STEPS - 1, step, 0)
    predict_stage()
    stage(Q, GQ, OQ, UQ, 1, correct, None, lambda: None, None, every=range(1, tiles - 1))
    local_part(1)

    def scaled(z, carry):
        for c in range(3):
            for r in range(inner):
                end_ref[c, z, pl.ds(8 * r, 8), :] = S[c, z + 1, pl.ds(HALO + 8 * r, 8), :] * (1.0 / damping)
        return carry

    lax.fori_loop(0, depth, scaled, 0)
    wave_part(1)
    x_part(0)
    y_part(0)
    last_part(0, mid_out)
    x_part(1)
    y_part(1)
    last_part(1, end_out)


def write_kernel(*refs):
    count = (len(refs) - 1) // 2
    copies = [pltpu.make_async_copy(refs[i], refs[count + i], refs[-1].at[i]) for i in range(count)]
    for copy in copies:
        copy.start()
    for copy in copies:
        copy.wait()


def phase_table(wave_count, total_length):
    index = np.arange(total_length)[:, None] * np.arange(wave_count)[None, :] % total_length
    phase = index * (2.0 * math.pi / total_length)
    return np.cos(phase), np.sin(phase)


def halves(table):
    big = table.astype(jnp.bfloat16)
    small = (table - big.astype(np.float64)).astype(jnp.bfloat16)
    return big, small


def wave_tables(depth, wide, lanes, nx, ny, nz):
    total_z = depth * nz
    owned = total_z // nx
    x_cos, x_sin = phase_table(KX, wide * nx)
    y_cos, y_sin = phase_table(KY, lanes * ny)
    z_cos, z_sin = phase_table(total_z, total_z)
    big, small = halves(np.concatenate([y_cos, y_sin, -y_sin, y_cos], 1).reshape(ny, lanes, 4 * KY))
    row = np.concatenate([big, small], 2)
    y_all = np.concatenate([row, row], 1)
    big, small = halves(np.concatenate([x_cos, x_sin], 1).reshape(nx, wide, 2 * KX).transpose(0, 2, 1))
    x_all = np.concatenate([big, big, small, small], 2)
    scale = float(wide * nx * lanes * ny * total_z) ** -0.5 / damping
    z_full = np.zeros((nz, nx, 8, nz, 2, depth))
    for first in range(nz):
        for place in range(nz):
            where = (first + place) % nz * depth + np.arange(depth)
            for p, (even, odd) in enumerate(((z_cos, -z_sin), (-z_sin, -z_cos))):
                for part, table in enumerate((even, odd)):
                    values = table[where].T.reshape(nx, owned, depth) * scale
                    z_full[first, :, p * owned : (p + 1) * owned, place, part] = values
    big, small = halves(z_full.reshape(nz, nx * 8, nz * 2 * depth))
    z_all = np.concatenate([big, big, small, small], 2)
    spread = np.zeros((2, lanes, depth, lanes))
    for z in range(depth):
        spread[:, 2 * HALO * z + HALO, z, 0] = 1.0
        spread[:, 2 * HALO * z + HALO - 1, z, lanes - 1] = 1.0
    spread_all = spread.reshape(2 * lanes, depth * lanes).astype(jnp.bfloat16)
    return jnp.asarray(y_all), jnp.asarray(x_all), jnp.asarray(z_all), jnp.asarray(spread_all)


def evolve(polar_angle, azimuth, classes, exchange_table):
    depth, wide, lanes = polar_angle.shape
    sizes = nx, ny, nz = (lax.axis_size("gx"), lax.axis_size("gy"), lax.axis_size("gz"))
    owned = depth * nz // nx
    half = KX // nz
    assert nz == 2 and depth * 2 * HALO == lanes and lanes == 4 * KY and 0 < 2 * owned <= 8
    ext = wide + 2 * HALO
    f32, i32, b16 = jnp.float32, jnp.int32, jnp.bfloat16
    hbm = pl.BlockSpec(memory_space=pltpu.HBM)
    anywhere = pl.BlockSpec(memory_space=pl.ANY)
    vmem = pl.BlockSpec(memory_space=pltpu.VMEM)
    V = pltpu.VMEM
    D = pltpu.SemaphoreType.DMA
    modes = jax.ShapeDtypeStruct((owned, 6 * KX * KY), f32)
    shapes = (jax.ShapeDtypeStruct((3, depth, wide, lanes), f32), modes, modes)
    results = pl.pallas_call(
        functools.partial(evolve_kernel, sizes),
        out_shape=shapes,
        in_specs=[hbm] * 7 + [pl.BlockSpec(memory_space=pltpu.SMEM)],
        out_specs=(vmem, vmem, vmem),
        scratch_shapes=[
            V((depth, wide, lanes), f32), V((depth, wide, lanes), f32), V((5, depth, wide, lanes), i32),
            V((3, depth + 2, ext, lanes), f32), V((3, depth + 2, ext, lanes), f32),
            V((4, depth + 1, ext, lanes), f32),
            V((3, ext, lanes), f32), V((3, ext, lanes), f32), V((4, ext, lanes), f32),
            V((3, ext, lanes), f32), V((3, ext, lanes), f32), V((ext, lanes), f32),
            V((2, depth, HALO, lanes), f32), V((2, depth, HALO, lanes), f32),
            V((4, depth, HALO, lanes), i32), V((4, depth, HALO, lanes), i32),
            V((5, wide, lanes), f32), V((5, ext, lanes), f32), V((5, ext, lanes), f32),
            V((3, ext, depth * lanes), f32), V((3, ext, depth * lanes), f32), V((3, ext, lanes), f32),
            V((2 * lanes, depth * lanes), b16),
            V((2 * lanes, 2 * lanes), b16), V((2 * KX, 4 * wide), b16), V((nx * 8, 8 * nz * depth), b16),
            V((depth * wide, 2 * lanes), b16), V((depth * KX, lanes), f32),
            V((2, nz, 3, 2 * depth, half * KY), f32), V((2, 3, 2 * depth, half * KY), f32),
            V((2, 3, nx, 8, half * KY), f32), V((2, 3, nx - 1, 8, half * KY), f32),
            V((2, 3, ny, 8, half * KY), f32), V((2, 3, nz, 8, half * KY), f32),
            D((8,)), D((8,)), D((6,)), D((6,)), D((4,)), D((4,)), D((3,)), D((3,)), D((9,)),
            D((2, 3)), D((2, 3)), D((2, 3, nx - 1)), D((2, 3, nx - 1)), D((2, 3, ny - 1)), D((2, 3, ny - 1)),
            D((2, 3)), D((2, 3)),
        ],
        compiler_params=pltpu.CompilerParams(collective_id=0, has_side_effects=True, vmem_limit_bytes=60000000),
        name="evolve",
    )(polar_angle, azimuth, classes, *wave_tables(depth, wide, lanes, nx, ny, nz), exchange_table)
    return pl.pallas_call(
        write_kernel,
        out_shape=shapes,
        in_specs=[vmem] * 3,
        out_specs=(anywhere,) * 3,
        scratch_shapes=[D((3,))],
        name="write",
    )(*results)


def solution(mesh):
    return jax.shard_map(
        evolve,
        mesh=mesh,
        in_specs=(
            P("gz", ("groups", "gx"), "gy"),
            P("gz", ("groups", "gx"), "gy"),
            P(None, "gz", ("groups", "gx"), "gy"),
            P(),
        ),
        out_specs=(
            P(None, "gz", ("groups", "gx"), "gy"),
            P(("groups", "gx"), None),
            P(("groups", "gx"), None),
        ),
        check_vma=False,
    )
```
